32 devices in a mesh: energy: 8 (over z, y), cell: 4 (over x, core).
Axes of the slice: x: 2, y: 2, z: 4, core: 2. Of those that a mesh axis runs over, the one named last changes fastest.
Arguments:
- retarded: bfloat16 [4, 2, 32, 256, 256], P('cell', None, 'energy'), may hold values from -0.25 to 0.25
- sigma_lesser: bfloat16 [4, 2, 32, 256, 256], P('cell', None, 'energy'), may hold values from -6 to 6
- sigma_greater: bfloat16 [4, 2, 32, 256, 256], P('cell', None, 'energy'), may hold values from -6 to 6
- coulomb: bfloat16 [4, 3, 256, 256], P('cell'), may hold values from -0.21875 to 0.21875
Outputs:
- screened: bfloat16 [4, 2, 32, 256, 256], P('cell', None, 'energy')
The draws below stay inside these ranges and needn't reach their ends.
All inputs are finite; a program needn't handle non-finite values.
Results may differ from the reference program's by a relative error of at most 0.009.
Values may be sent and summed in bfloat16 or wider, within the bound.
A program may use at most 64 MiB of HBM per device.

```python
import math
import jax
import jax.numpy as jnp
from jax import lax

NORB = 256
NE = 32
CELLS = 4


def levels(rng, shape, pieces, low, high):
    def one(position, parts):
        heights = jax.random.uniform(jax.random.fold_in(jax.random.fold_in(rng, 6), position), (parts,), jnp.float32, low / len(pieces), high / len(pieces))
        return jnp.repeat(jnp.exp(heights), shape[position] // parts).reshape((-1,) + (1,) * (len(shape) - position - 1))

    level = one(*pieces[0])
    for cut in pieces[1:]:
        level = level * one(*cut)
    return level


def noise(key, shape, width, limit, pieces=(), held_as=jnp.bfloat16):
    drawn = width * jax.random.normal(key, shape, jnp.float32)
    if pieces:
        drawn = drawn * levels(key, shape, pieces, -0.22, 0.18)
    return jnp.clip(drawn, -limit, limit).astype(held_as)


def setup_inputs(seed: int = 0) -> dict:
    keys = jax.random.split(jax.random.key(seed), 5)
    return {
        "retarded": noise(keys[0], (CELLS, 2, NE, NORB, NORB), (2 * NORB) ** -0.5, 0.25, ((0, 4), (2, 8))),
        "sigma_lesser": noise(keys[1], (CELLS, 2, NE, NORB, NORB), 1.0, 6.0, ((0, 4), (2, 8))),
        "sigma_greater": noise(keys[2], (CELLS, 2, NE, NORB, NORB), 1.0, 6.0, ((0, 4), (2, 8))),
        "coulomb": noise(keys[3], (CELLS, 3, NORB, NORB), (3 * NORB) ** -0.5, 0.21875, ((0, 4),)),
    }


def complex_product(first_re, first_im, second_re, second_im):
    first_re = first_re.astype(jnp.float32)
    first_im = first_im.astype(jnp.float32)
    second_re = second_re.astype(jnp.float32)
    second_im = second_im.astype(jnp.float32)
    real_part = jnp.einsum('eik,ekj->eij', first_re, second_re) - jnp.einsum('eik,ekj->eij', first_im, second_im)
    imag_part = jnp.einsum('eik,ekj->eij', first_re, second_im) + jnp.einsum('eik,ekj->eij', first_im, second_re)
    return (real_part.astype(jnp.bfloat16), imag_part.astype(jnp.bfloat16))

def adjoint_product(first_re, first_im, green_re, green_im):
    first_re = first_re.astype(jnp.float32)
    first_im = first_im.astype(jnp.float32)
    green_re = green_re.astype(jnp.float32)
    green_im = green_im.astype(jnp.float32)
    real_part = jnp.einsum('eik,ejk->eij', first_re, green_re) + jnp.einsum('eik,ejk->eij', first_im, green_im)
    imag_part = jnp.einsum('eik,ejk->eij', first_im, green_re) - jnp.einsum('eik,ejk->eij', first_re, green_im)
    return jnp.stack([real_part, imag_part]).astype(jnp.bfloat16)

def triple(green, sigma):
    half_re, half_im = complex_product(green[0], green[1], sigma[0], sigma[1])
    return adjoint_product(half_re, half_im, green[0], green[1])

def tables(energies):
    length = 2 * energies
    frequency = lax.broadcasted_iota(jnp.int32, (length, energies), 0)
    energy_index = lax.broadcasted_iota(jnp.int32, (length, energies), 1)
    angles = 2.0 * math.pi / length * (frequency * energy_index % length).astype(jnp.float32)
    cos_table = jnp.cos(angles)
    sin_table = jnp.sin(angles)
    forward_first = jnp.concatenate([jnp.concatenate([cos_table, sin_table], 1), jnp.concatenate([-sin_table, cos_table], 1)], 0)
    forward_second = jnp.concatenate([jnp.concatenate([cos_table, -sin_table], 1), jnp.concatenate([sin_table, cos_table], 1)], 0)
    factor = 1.0 / (length * math.sqrt(energies))
    inverse = jnp.concatenate([jnp.concatenate([cos_table.T, -sin_table.T], 1), jnp.concatenate([sin_table.T, cos_table.T], 1)], 0) * factor
    return (forward_first.astype(jnp.bfloat16), forward_second.astype(jnp.bfloat16), inverse.astype(jnp.bfloat16))

def correlate(lesser, mirrored):
    energies = lesser.shape[1]
    length = 2 * energies
    elements = lesser.shape[2] * lesser.shape[3]
    forward_first, forward_second, inverse = tables(energies)
    first_flat = lesser.reshape(2 * energies, elements)
    second_flat = mirrored.reshape(2 * energies, elements)
    spec_first = jnp.dot(forward_first, first_flat, preferred_element_type=jnp.float32)
    spec_second = jnp.dot(forward_second, second_flat, preferred_element_type=jnp.float32)
    left_re, left_im = (spec_first[:length], spec_first[length:])
    right_re, right_im = (spec_second[:length], spec_second[length:])
    product = jnp.concatenate([left_re * right_re - left_im * right_im, left_re * right_im + left_im * right_re], 0).astype(jnp.bfloat16)
    lag_values = jnp.dot(inverse, product, preferred_element_type=jnp.float32)
    return lag_values.reshape(lesser.shape).astype(jnp.bfloat16)

def reference(retarded, sigma_lesser, sigma_greater, coulomb):
    polarized = []
    for cell_index in range(CELLS):
        lesser = triple(retarded[cell_index], sigma_lesser[cell_index])
        greater = triple(retarded[cell_index], sigma_greater[cell_index])
        polarized.append(correlate(lesser, jnp.swapaxes(greater, -1, -2)))
    outputs = []
    for cell_index in range(CELLS):
        summed = jnp.zeros((2, NE, NORB, NORB), jnp.float32)
        for offset in (-1, 0, 1):
            neighbour = cell_index + offset
            if 0 <= neighbour < CELLS:
                weights = coulomb[cell_index, offset + 1].astype(jnp.float32)
                summed = summed + jnp.einsum('ik,cekj->ceij', weights, polarized[neighbour].astype(jnp.float32))
        outputs.append(summed.astype(jnp.bfloat16))
    return jnp.stack(outputs)
```

```python
import functools
import math

import jax
import jax.numpy as jnp
from jax import lax
from jax.experimental import pallas as pl
from jax.experimental.pallas import tpu as pltpu
from jax.sharding import PartitionSpec as P

MESH = pl.DeviceIdType.MESH
ROWS = 16
LANES = 128
QUARTERS = 4
LESSER, GREATER = 0, 1
AHEAD = 4
SHIFT = 6
LOW_LAG = 1
DONE_LAG = 2
LATE = 3
F32 = jnp.float32
BF16 = jnp.bfloat16


def nn(a, b):
    return jnp.dot(a, b, preferred_element_type=F32)


def nt(a, b):
    return lax.dot_general(a, b, (((1,), (1,)), ((), ())), preferred_element_type=F32)


def fused_kernel(
    n, cells, green_in, sig_l_in, sig_g_in, coulomb_in, out,
    green, sig_l, sig_g, coulomb, send, recv, send_p, low, pol, total,
    in_sem, coulomb_sem, sent_sem, arrive_sem, done_sem, halo_send_sem, halo_recv_sem,
):
    me = lax.axis_index("energy")
    cell = lax.axis_index("cell")
    local = green.shape[1]
    norb = green.shape[2]
    width = n // QUARTERS
    half = 2 * width
    quarter, place = me // width, lax.rem(me, width)
    home = jnp.where(quarter == 0, 1, 2)
    strip = norb // width
    row_parts = strip // ROWS
    col_parts = norb // LANES
    chunks = row_parts * col_parts
    has_low = cell > 0
    has_high = cell < cells - 1
    offset = {LESSER: 0, GREATER: n + 1}

    def load(i, e):
        source, held = ((green_in, green), (sig_g_in, sig_g), (sig_l_in, sig_l))[i]
        return pltpu.make_async_copy(source.at[:, e], held.at[:, e], in_sem.at[i, e])

    for e in range(local):
        load(0, e).start()
        load(1, e).start()

    barrier = pltpu.get_barrier_semaphore()

    def greet(other):
        pl.semaphore_signal(barrier, inc=1, device_id={"energy": other}, device_id_type=MESH)

    @pl.loop(1, width)
    def _(k):
        greet(quarter * width + lax.rem(place + k, width))

    @pl.when(quarter == 2)
    def _():
        greet(width + place)
        greet(3 * width + place)

    @pl.when(quarter == 1)
    def _():
        greet(place)

    @pl.when(quarter == 0)
    def _():
        @pl.loop(0, width)
        def _(k):
            greet(width + k)

    @pl.when(quarter != 2)
    def _():
        @pl.loop(0, width)
        def _(k):
            greet(2 * width + k)

    @pl.when(has_low)
    def _():
        pl.semaphore_signal(barrier, inc=1, device_id={"cell": cell - 1}, device_id_type=MESH)

    @pl.when(has_high)
    def _():
        pl.semaphore_signal(barrier, inc=1, device_id={"cell": cell + 1}, device_id_type=MESH)

    for e in range(local):
        load(2, e).start()
    coulomb_load = pltpu.make_async_copy(coulomb_in, coulomb, coulomb_sem)
    coulomb_load.start()

    def put(value, kind, comp, e):
        value = value.astype(BF16).reshape(width, strip, norb)
        for q in range(chunks):
            c, r = divmod(q, row_parts)
            send[kind, q, :, comp, e] = value[:, r * ROWS:(r + 1) * ROWS, c * LANES:(c + 1) * LANES]

    @pl.loop(0, local)
    def _(e):
        load(0, e).wait()
        load(1, e).wait()
        g_re, g_im = green[0, e], green[1, e]
        s_re, s_im = sig_g[0, e], sig_g[1, e]
        half_re = (nn(g_re, s_re) - nn(g_im, s_im)).astype(BF16)
        half_im = (nn(g_re, s_im) + nn(g_im, s_re)).astype(BF16)
        put(nt(g_re, half_re) + nt(g_im, half_im), GREATER, 0, e)
        put(nt(g_re, half_im) - nt(g_im, half_re), GREATER, 1, e)

    reach = jnp.where(quarter == 1, width + 1, jnp.where(quarter == 2, 3 * width, 1))
    pl.semaphore_wait(barrier, width - 1 + reach + has_low.astype(jnp.int32) + has_high.astype(jnp.int32))

    def sum_of(count):
        return recv.at[0, 0:count]

    def block_copy(source, kind, q, slot, other, lane):
        return pltpu.make_async_remote_copy(
            src_ref=source, dst_ref=recv.at[q, offset[kind] + slot],
            send_sem=sent_sem.at[q], recv_sem=arrive_sem.at[lane, q],
            device_id={"energy": other}, device_id_type=MESH,
        )

    def exchange(kind, q):
        lane = jnp.where(quarter == 2, 0, 0 if kind == GREATER else 1)

        @pl.loop(1, width)
        def _(k):
            where = lax.rem(place + k, width)
            block_copy(send.at[kind, q, where], kind, q, me, quarter * width + where, lane).start()

    def lane_at_home(kind):
        return jnp.where(quarter == 0, 2 if kind == GREATER else 1, 0)

    def forward_own(kind, q):
        block_copy(send.at[kind, q, place], kind, q, me, home * width + place, lane_at_home(kind)).start()

    def forward_others(kind, q):
        @pl.loop(1, width)
        def _(k):
            slot = quarter * width + lax.rem(place + k, width)
            block_copy(recv.at[q, offset[kind] + slot], kind, q, slot, home * width + place, lane_at_home(kind)).start()

    def arrived(lane, q, count):
        pltpu.make_async_copy(sum_of(count), sum_of(count), arrive_sem.at[lane, q]).wait()

    ahead = min(AHEAD, chunks)

    @pl.when(quarter != 2)
    def _():
        @pl.loop(0, ahead)
        def _(q):
            forward_own(GREATER, q)

    @pl.loop(0, ahead)
    def _(q):
        exchange(GREATER, q)

    @pl.loop(0, local)
    def _(e):
        load(2, e).wait()
        g_re, g_im = green[0, e], green[1, e]
        l_re, l_im = sig_l[0, e], sig_l[1, e]
        half_re = (nn(g_re, l_re) - nn(g_im, l_im)).astype(BF16)
        half_im = (nn(g_re, l_im) + nn(g_im, l_re)).astype(BF16)
        put(nt(half_re, g_re) + nt(half_im, g_im), LESSER, 0, e)
        put(nt(half_im, g_re) - nt(half_re, g_im), LESSER, 1, e)

    @pl.when(quarter == 3)
    def _():
        @pl.loop(0, ahead)
        def _(q):
            forward_own(LESSER, q)

    @pl.loop(0, ahead)
    def _(q):
        exchange(LESSER, q)

    @pl.loop(ahead, chunks)
    def _(q):
        exchange(GREATER, q)
        exchange(LESSER, q)

    blank = jnp.zeros((2, local, ROWS, LANES), BF16)

    @pl.when(jnp.logical_or(quarter == 1, quarter == 2))
    def _():
        @pl.loop(0, chunks)
        def _(q):
            for kind in (LESSER, GREATER):
                recv[q, offset[kind] + me] = send[kind, q, place]

    @pl.when(quarter == 1)
    def _():
        @pl.loop(0, chunks)
        def _(q):
            recv[q, half] = blank

    @pl.when(quarter == 2)
    def _():
        @pl.loop(0, chunks)
        def _(q):
            recv[q, half - 1] = blank
            recv[q, n] = blank

    def spot(q):
        rows = pl.ds(pl.multiple_of(lax.rem(q, row_parts) * ROWS, ROWS), ROWS)
        return rows, pl.ds(pl.multiple_of(q // row_parts * LANES, LANES), LANES)

    def return_copy(q, owner):
        return pltpu.make_async_remote_copy(
            src_ref=send_p.at[q, owner], dst_ref=pol.at[1, :, :, place, *spot(q)],
            send_sem=sent_sem.at[q], recv_sem=done_sem.at[q],
            device_id={"energy": owner}, device_id_type=MESH,
        )

    def low_copy(q, owner):
        return pltpu.make_async_remote_copy(
            src_ref=send_p.at[q, owner], dst_ref=low.at[q, place],
            send_sem=sent_sem.at[q], recv_sem=done_sem.at[q],
            device_id={"energy": owner}, device_id_type=MESH,
        )

    def halo_copy(q, slot, other):
        return pltpu.make_async_remote_copy(
            src_ref=pol.at[1, :, :, :, *spot(q)], dst_ref=pol.at[slot, :, :, :, *spot(q)],
            send_sem=halo_send_sem.at[slot // 2], recv_sem=halo_recv_sem.at[slot // 2, q // row_parts],
            device_id={"cell": other}, device_id_type=MESH,
        )

    factor = 1.0 / math.sqrt(n * local)

    def correlate(q, b, first_step, last_step):
        def step(a, acc):
            first = [
                (recv[q, a + b + i // local, 0, i % local].astype(F32), recv[q, a + b + i // local, 1, i % local].astype(F32))
                for i in range(2 * local - 1)
            ]
            acc = list(acc)
            for e in range(local):
                x_re, x_im = recv[q, n + 1 + a, 0, e].astype(F32), recv[q, n + 1 + a, 1, e].astype(F32)
                for w in range(local):
                    y_re, y_im = first[e + w]
                    acc[2 * w] = acc[2 * w] + (y_re * x_re - y_im * x_im)
                    acc[2 * w + 1] = acc[2 * w + 1] + (y_re * x_im + y_im * x_re)
            return tuple(acc)

        zero = jnp.zeros((ROWS, LANES), F32)
        acc = lax.fori_loop(first_step, last_step, step, (zero,) * (2 * local))
        for w in range(local):
            send_p[q, b, 0, w] = (acc[2 * w] * factor).astype(BF16)
            send_p[q, b, 1, w] = (acc[2 * w + 1] * factor).astype(BF16)

    def halo(q):
        @pl.when(has_low)
        def _():
            halo_copy(q, 2, cell - 1).start()

        @pl.when(has_high)
        def _():
            halo_copy(q, 0, cell + 1).start()

    def done(q, count):
        pltpu.make_async_copy(sum_of(count), sum_of(count), done_sem.at[q]).wait()

    def finish(q, count):
        done(q, count)

        @pl.loop(0, width)
        def _(where):
            for c in range(2):
                for w in range(local):
                    place_of = (1, c, w, where, *spot(q))
                    pol[place_of] = (pol[place_of].astype(F32) + low[q, where, c, w].astype(F32)).astype(BF16)

        halo(q)

    @pl.when(jnp.logical_not(has_low))
    def _():
        pol[0] = jnp.zeros_like(pol[0])

    @pl.when(jnp.logical_not(has_high))
    def _():
        pol[2] = jnp.zeros_like(pol[2])

    @pl.when(quarter == 0)
    def _():
        @pl.loop(0, chunks + SHIFT)
        def _(t):
            @pl.when(t < chunks)
            def _():
                if width > 1:
                    arrived(0, t, width - 1)
                forward_others(GREATER, t)

            @pl.when(t + ahead < chunks)
            def _():
                forward_own(GREATER, t + ahead)

            @pl.when(t >= SHIFT)
            def _():
                q = t - SHIFT
                forward_own(LESSER, q)
                if width > 1:
                    arrived(1, q, width - 1)
                forward_others(LESSER, q)

        @pl.loop(0, chunks)
        def _(q):
            finish(q, 2 * width)

    @pl.when(quarter == 1)
    def _():
        @pl.loop(0, chunks + SHIFT + LOW_LAG + DONE_LAG)
        def _(t):
            @pl.when(t < chunks)
            def _():
                if width > 1:
                    arrived(0, t, width - 1)
                forward_others(GREATER, t)
                arrived(2, t, width)
                lower = recv.at[t, n + 1:n + 1 + width]
                pltpu.make_async_remote_copy(
                    src_ref=lower, dst_ref=lower, send_sem=sent_sem.at[t], recv_sem=arrive_sem.at[0, t],
                    device_id={"energy": 2 * width + place}, device_id_type=MESH,
                ).start()

            @pl.when(t + ahead < chunks)
            def _():
                forward_own(GREATER, t + ahead)

            late = SHIFT + LOW_LAG

            @pl.when(jnp.logical_and(t >= late, t < chunks + late))
            def _():
                q = t - late
                arrived(1, q, 2 * width - 1)

                @pl.loop(0, half)
                def _(b):
                    correlate(q, b, 0, half - b)

                    @pl.when(b != me)
                    def _():
                        low_copy(q, b).start()

                    @pl.when(b == me)
                    def _():
                        low[q, place] = send_p[q, b]

            @pl.when(t >= late + DONE_LAG)
            def _():
                finish(t - late - DONE_LAG, 2 * width - 1)

    @pl.when(quarter == 2)
    def _():
        @pl.loop(0, chunks + LATE)
        def _(t):
            @pl.when(t < chunks)
            def _():
                arrived(0, t, 6 * width - 2)

                @pl.loop(0, n)
                def _(b):
                    correlate(t, b, jnp.maximum(half - 1 - b, 0), n - b)

                    @pl.when(b != me)
                    def _():
                        return_copy(t, b).start()

                    @pl.when(b == me)
                    def _():
                        pol[1, :, :, place, *spot(t)] = send_p[t, b]

            @pl.when(t >= LATE)
            def _():
                if width > 1:
                    done(t - LATE, width - 1)
                halo(t - LATE)

    @pl.when(quarter == 3)
    def _():
        @pl.loop(0, chunks)
        def _(t):
            for kind in (GREATER, LESSER):
                if width > 1:
                    arrived(0 if kind == GREATER else 1, t, width - 1)
                forward_others(kind, t)

            @pl.when(t + ahead < chunks)
            def _():
                forward_own(GREATER, t + ahead)
                forward_own(LESSER, t + ahead)

        @pl.loop(0, chunks)
        def _(q):
            done(q, width)
            halo(q)

    coulomb_load.wait()

    def polarized(slot, c, e, part):
        return pol[slot, c, e, :, :, part * LANES:(part + 1) * LANES].reshape(norb, LANES)

    @pl.loop(0, local)
    def _(e):
        for c in range(2):
            for part in range(col_parts):
                total[c, e, :, part * LANES:(part + 1) * LANES] = nn(coulomb[1], polarized(1, c, e, part))

    for part in range(col_parts):
        group = (slice(None), slice(None), slice(None), slice(None), slice(part * LANES, (part + 1) * LANES))

        @pl.when(has_low)
        def _():
            pltpu.make_async_copy(pol.at[0, *group], pol.at[0, *group], halo_recv_sem.at[0, part]).wait()

        @pl.when(has_high)
        def _():
            pltpu.make_async_copy(pol.at[2, *group], pol.at[2, *group], halo_recv_sem.at[1, part]).wait()

        @pl.loop(0, local)
        def _(e):
            for c in range(2):
                summed = total[c, e, :, part * LANES:(part + 1) * LANES]
                summed = summed + nn(coulomb[0], polarized(0, c, e, part)) + nn(coulomb[2], polarized(2, c, e, part))
                out[c, e, :, part * LANES:(part + 1) * LANES] = summed.astype(BF16)

    @pl.when(has_low)
    def _():
        pltpu.make_async_copy(pol.at[1], pol.at[1], halo_send_sem.at[1]).wait()

    @pl.when(has_high)
    def _():
        pltpu.make_async_copy(pol.at[1], pol.at[1], halo_send_sem.at[0]).wait()

    def all_sent(count):
        @pl.loop(0, chunks)
        def _(q):
            pltpu.make_async_copy(sum_of(count), sum_of(count), sent_sem.at[q]).wait()

    @pl.when(jnp.logical_or(quarter == 0, quarter == 3))
    def _():
        all_sent(4 * width - 2)

    @pl.when(jnp.logical_or(quarter == 1, quarter == 2))
    def _():
        all_sent(6 * width - 3)


def fused(n, cells, retarded, sigma_lesser, sigma_greater, coulomb):
    green = retarded[0]
    local, norb = green.shape[1], green.shape[2]
    width = n // QUARTERS
    strip = norb // width
    chunks = strip // ROWS * (norb // LANES)
    dma = pltpu.SemaphoreType.DMA
    result = pl.pallas_call(
        functools.partial(fused_kernel, n, cells),
        out_shape=pltpu.VMEM(green.shape, BF16),
        in_specs=[pl.BlockSpec(memory_space=pltpu.HBM)] * 4,
        out_specs=pl.BlockSpec(memory_space=pltpu.VMEM),
        scratch_shapes=[
            pltpu.VMEM(green.shape, BF16),
            pltpu.VMEM(green.shape, BF16),
            pltpu.VMEM(green.shape, BF16),
            pltpu.VMEM(coulomb.shape[1:], BF16),
            pltpu.VMEM((2, chunks, width, 2, local, ROWS, LANES), BF16),
            pltpu.VMEM((chunks, 2 * n + 1, 2, local, ROWS, LANES), BF16),
            pltpu.VMEM((chunks, n, 2, local, ROWS, LANES), BF16),
            pltpu.VMEM((chunks, width, 2, local, ROWS, LANES), BF16),
            pltpu.VMEM((3, 2, local, width, strip, norb), BF16),
            pltpu.VMEM((2, local, norb, norb), F32),
            dma((3, local)), dma,
            dma((chunks,)), dma((3, chunks)), dma((chunks,)),
            dma((2,)), dma((2, norb // LANES)),
        ],
        compiler_params=pltpu.CompilerParams(
            collective_id=0, has_side_effects=True, vmem_limit_bytes=56 * 1024 * 1024
        ),
    )(green, sigma_lesser[0], sigma_greater[0], coulomb[0])
    return result[None]


def thin(n, cells, retarded, sigma_lesser, sigma_greater, coulomb):
    green = retarded[0]
    local = green.shape[1]

    def halves(sigma):
        def product(x, y):
            return jnp.einsum("eik,ekj->eij", x, y, preferred_element_type=F32)

        re = product(green[0], sigma[0]) - product(green[1], sigma[1])
        im = product(green[0], sigma[1]) + product(green[1], sigma[0])
        return re.astype(BF16), im.astype(BF16)

    def adjoint(x, y):
        return jnp.einsum("eik,ejk->eij", x, y, preferred_element_type=F32)

    re, im = halves(sigma_lesser[0])
    lesser = jnp.stack([adjoint(re, green[0]) + adjoint(im, green[1]), adjoint(im, green[0]) - adjoint(re, green[1])])
    re, im = halves(sigma_greater[0])
    greater = jnp.stack([adjoint(green[0], re) + adjoint(green[1], im), adjoint(green[0], im) - adjoint(green[1], re)])
    first = lax.all_to_all(lesser.astype(BF16), "energy", split_axis=2, concat_axis=1, tiled=True).astype(F32)
    second = lax.all_to_all(greater.astype(BF16), "energy", split_axis=2, concat_axis=1, tiled=True).astype(F32)
    energies = n * local
    padded = jnp.concatenate([first, jnp.zeros_like(first)], axis=1)

    def lag(w):
        y = lax.dynamic_slice_in_dim(padded, w, energies, axis=1)
        re = jnp.sum(y[0] * second[0] - y[1] * second[1], axis=0)
        im = jnp.sum(y[0] * second[1] + y[1] * second[0], axis=0)
        return (jnp.stack([re, im]) / math.sqrt(energies)).astype(BF16)

    polarized = jnp.swapaxes(lax.map(lag, jnp.arange(energies)), 0, 1)
    polarized = lax.all_to_all(polarized, "energy", split_axis=1, concat_axis=2, tiled=True)
    up = [(i, i + 1) for i in range(cells - 1)]
    low = lax.ppermute(polarized, "cell", up)
    high = lax.ppermute(polarized, "cell", [(t, s) for s, t in up])
    stacked = jnp.stack([low, polarized, high])
    summed = jnp.einsum("dik,dcekj->ceij", coulomb[0], stacked, preferred_element_type=F32)
    return summed.astype(BF16)[None]


def solution(mesh):
    n, cells = mesh.shape["energy"], mesh.shape["cell"]

    def on_device(retarded, sigma_lesser, sigma_greater, coulomb):
        norb = retarded.shape[-1]
        whole_tiles = n % QUARTERS == 0 and norb % LANES == 0 and norb % (n // QUARTERS * ROWS) == 0
        plan = fused if whole_tiles else thin
        return plan(n, cells, retarded, sigma_lesser, sigma_greater, coulomb)

    in_specs = (
        P("cell", None, "energy", None, None),
        P("cell", None, "energy", None, None),
        P("cell", None, "energy", None, None),
        P("cell", None, None, None),
    )
    out_specs = P("cell", None, "energy", None, None)
    return jax.shard_map(
        on_device, mesh=mesh, in_specs=in_specs, out_specs=out_specs, check_vma=False
    )
```

```python
import functools
import math

import jax
import jax.numpy as jnp
from jax import lax
from jax.experimental import pallas as pl
from jax.experimental.pallas import tpu as pltpu
from jax.sharding import PartitionSpec as P

MESH = pl.DeviceIdType.MESH
ROWS = 16
LANES = 128
QUARTERS = 4
LESSER, GREATER = 0, 1
DIRECT = 1
AHEAD = 4
AHEAD_TOP = 2
EARLY = 4
SHIFT = 1
LOW_LAG = 0
DONE_LAG = 6
LATE = 3
F32 = jnp.float32
BF16 = jnp.bfloat16


def nn(a, b):
    return jnp.dot(a, b, preferred_element_type=F32)


def nt(a, b):
    return lax.dot_general(a, b, (((1,), (1,)), ((), ())), preferred_element_type=F32)


def fused_kernel(
    n, cells, green_in, sig_l_in, sig_g_in, coulomb_in, out,
    green, sig_l, sig_g, coulomb, send, recv, send_p, low, pol, total,
    in_sem, coulomb_sem, sent_sem, arrive_sem, done_sem, halo_send_sem, halo_recv_sem,
):
    me = lax.axis_index("energy")
    cell = lax.axis_index("cell")
    local = green.shape[1]
    norb = green.shape[2]
    width = n // QUARTERS
    half = 2 * width
    quarter, place = me // width, lax.rem(me, width)
    home = jnp.where(quarter == 0, 1, 2)
    strip = norb // width
    row_parts = strip // ROWS
    col_parts = norb // LANES
    chunks = row_parts * col_parts
    straight = min(DIRECT, chunks)
    has_low = cell > 0
    has_high = cell < cells - 1
    offset = {LESSER: 0, GREATER: n + 1}

    def batch(q):
        return jnp.where(q < straight, 0, 1)

    def load(i, e):
        source, held = ((green_in, green), (sig_g_in, sig_g), (sig_l_in, sig_l))[i]
        return pltpu.make_async_copy(source.at[:, e], held.at[:, e], in_sem.at[i, e])

    for e in range(local):
        load(0, e).start()
        load(1, e).start()

    barrier = pltpu.get_barrier_semaphore()

    def greet(other):
        pl.semaphore_signal(barrier, inc=1, device_id={"energy": other}, device_id_type=MESH)

    @pl.loop(1, width)
    def _(k):
        greet(quarter * width + lax.rem(place + k, width))

    def greet_quarter(other):
        @pl.loop(0, width)
        def _(k):
            greet(other * width + k)

    for mine, others in ((0, (1, 2)), (1, (0, 2)), (2, (1, 3)), (3, (2,))):
        @pl.when(quarter == mine)
        def _():
            for other in others:
                greet_quarter(other)

    @pl.when(has_low)
    def _():
        pl.semaphore_signal(barrier, inc=1, device_id={"cell": cell - 1}, device_id_type=MESH)

    @pl.when(has_high)
    def _():
        pl.semaphore_signal(barrier, inc=1, device_id={"cell": cell + 1}, device_id_type=MESH)

    for e in range(local):
        load(2, e).start()
    coulomb_load = pltpu.make_async_copy(coulomb_in, coulomb, coulomb_sem)
    coulomb_load.start()

    def put(value, kind, comp, e):
        value = value.astype(BF16).reshape(width, strip, norb)
        for q in range(chunks):
            c, r = divmod(q, row_parts)
            send[kind, q, :, comp, e] = value[:, r * ROWS:(r + 1) * ROWS, c * LANES:(c + 1) * LANES]

    @pl.loop(0, local)
    def _(e):
        load(0, e).wait()
        load(1, e).wait()
        g_re, g_im = green[0, e], green[1, e]
        s_re, s_im = sig_g[0, e], sig_g[1, e]
        g_neg = -g_im
        half_re = (nn(g_re, s_re) + nn(g_neg, s_im)).astype(BF16)
        half_im = (nn(g_re, s_im) + nn(g_im, s_re)).astype(BF16)
        put(nt(g_re, half_re) + nt(g_im, half_im), GREATER, 0, e)
        put(nt(g_re, half_im) + nt(g_neg, half_re), GREATER, 1, e)

    reach = width * jnp.where(quarter == 1, 2, jnp.where(quarter == 2, 3, 1))
    pl.semaphore_wait(barrier, width - 1 + reach + has_low.astype(jnp.int32) + has_high.astype(jnp.int32))

    def sum_of(count):
        return recv.at[0, 0:count]

    def block_copy(source, kind, q, slot, other, lane):
        return pltpu.make_async_remote_copy(
            src_ref=source, dst_ref=recv.at[q, offset[kind] + slot],
            send_sem=sent_sem.at[batch(q)], recv_sem=arrive_sem.at[lane, q],
            device_id={"energy": other}, device_id_type=MESH,
        )

    def exchange(kind, q):
        lane = jnp.where(quarter == 2, 0, 0 if kind == GREATER else 1)

        @pl.loop(1, width)
        def _(k):
            where = lax.rem(place + k, width)
            block_copy(send.at[kind, q, where], kind, q, me, quarter * width + where, lane).start()

    def lane_at_home(kind):
        return jnp.where(quarter == 0, 2 if kind == GREATER else 1, 0)

    def forward_own(kind, q):
        block_copy(send.at[kind, q, place], kind, q, me, home * width + place, lane_at_home(kind)).start()

    def forward_others(kind, q):
        @pl.loop(1, width)
        def _(k):
            slot = quarter * width + lax.rem(place + k, width)
            block_copy(recv.at[q, offset[kind] + slot], kind, q, slot, home * width + place, lane_at_home(kind)).start()

    def arrived(lane, q, count):
        pltpu.make_async_copy(sum_of(count), sum_of(count), arrive_sem.at[lane, q]).wait()

    def direct(kind, q):
        @pl.loop(0, width)
        def _(where):
            block_copy(send.at[kind, q, where], kind, q, me, home * width + where, lane_at_home(kind)).start()

    ahead = jnp.where(quarter == 3, min(AHEAD_TOP, chunks), min(AHEAD, chunks))
    first = jnp.where(quarter == 3, straight, 0)

    @pl.when(jnp.logical_or(quarter == 1, quarter == 3))
    def _():
        @pl.loop(0, straight)
        def _(q):
            direct(GREATER, q)

    @pl.when(quarter != 2)
    def _():
        @pl.loop(jnp.where(quarter == 0, 0, straight), ahead)
        def _(q):
            forward_own(GREATER, q)

    @pl.loop(first, ahead)
    def _(q):
        exchange(GREATER, q)

    @pl.loop(0, local)
    def _(e):
        load(2, e).wait()
        g_re, g_im = green[0, e], green[1, e]
        l_re, l_im = sig_l[0, e], sig_l[1, e]
        g_neg = -g_im
        half_re = (nn(g_re, l_re) + nn(g_neg, l_im)).astype(BF16)
        half_im = (nn(g_re, l_im) + nn(g_im, l_re)).astype(BF16)
        put(nt(half_re, g_re) + nt(half_im, g_im), LESSER, 0, e)
        put(nt(half_im, g_re) + nt(half_re, g_neg), LESSER, 1, e)

    @pl.when(quarter == 3)
    def _():
        @pl.loop(0, straight)
        def _(q):
            direct(LESSER, q)

        @pl.loop(straight, ahead)
        def _(q):
            forward_own(LESSER, q)

    @pl.loop(first, ahead)
    def _(q):
        exchange(LESSER, q)

    @pl.loop(ahead, jnp.where(jnp.logical_or(quarter == 1, quarter == 2), min(EARLY, chunks), chunks))
    def _(q):
        exchange(GREATER, q)
        exchange(LESSER, q)

    def more(t):
        @pl.when(t + EARLY < chunks)
        def _():
            exchange(GREATER, t + EARLY)
            exchange(LESSER, t + EARLY)

    blank = jnp.zeros((2, local, ROWS, LANES), BF16)

    @pl.when(jnp.logical_or(quarter == 1, quarter == 2))
    def _():
        @pl.loop(0, chunks)
        def _(q):
            for kind in (LESSER, GREATER):
                recv[q, offset[kind] + me] = send[kind, q, place]

    @pl.when(quarter == 1)
    def _():
        @pl.loop(0, chunks)
        def _(q):
            recv[q, half] = blank

    @pl.when(quarter == 2)
    def _():
        @pl.loop(0, chunks)
        def _(q):
            recv[q, half - 1] = blank
            recv[q, n] = blank

    def spot(q):
        rows = pl.ds(pl.multiple_of(lax.rem(q, row_parts) * ROWS, ROWS), ROWS)
        return rows, pl.ds(pl.multiple_of(q // row_parts * LANES, LANES), LANES)

    def return_copy(q, owner):
        return pltpu.make_async_remote_copy(
            src_ref=send_p.at[q, owner], dst_ref=pol.at[1, :, :, place, *spot(q)],
            send_sem=sent_sem.at[batch(q)], recv_sem=done_sem.at[q],
            device_id={"energy": owner}, device_id_type=MESH,
        )

    def low_copy(q, owner):
        return pltpu.make_async_remote_copy(
            src_ref=send_p.at[q, owner], dst_ref=low.at[q, place],
            send_sem=sent_sem.at[batch(q)], recv_sem=done_sem.at[q],
            device_id={"energy": owner}, device_id_type=MESH,
        )

    def halo_copy(q, slot, other):
        return pltpu.make_async_remote_copy(
            src_ref=pol.at[1, :, :, :, *spot(q)], dst_ref=pol.at[slot, :, :, :, *spot(q)],
            send_sem=halo_send_sem.at[slot // 2], recv_sem=halo_recv_sem.at[slot // 2, q // row_parts],
            device_id={"cell": other}, device_id_type=MESH,
        )

    factor = 1.0 / math.sqrt(n * local)

    def correlate(q, b, first_step, last_step):
        def step(a, acc):
            first = [
                (recv[q, a + b + i // local, 0, i % local].astype(F32), recv[q, a + b + i // local, 1, i % local].astype(F32))
                for i in range(2 * local - 1)
            ]
            acc = list(acc)
            for e in range(local):
                x_re, x_im = recv[q, n + 1 + a, 0, e].astype(F32), recv[q, n + 1 + a, 1, e].astype(F32)
                for w in range(local):
                    y_re, y_im = first[e + w]
                    acc[2 * w] = acc[2 * w] + (y_re * x_re - y_im * x_im)
                    acc[2 * w + 1] = acc[2 * w + 1] + (y_re * x_im + y_im * x_re)
            return tuple(acc)

        zero = jnp.zeros((ROWS, LANES), F32)
        acc = lax.fori_loop(first_step, last_step, step, (zero,) * (2 * local))
        for w in range(local):
            send_p[q, b, 0, w] = (acc[2 * w] * factor).astype(BF16)
            send_p[q, b, 1, w] = (acc[2 * w + 1] * factor).astype(BF16)

    def halo(q):
        @pl.when(has_low)
        def _():
            halo_copy(q, 2, cell - 1).start()

        @pl.when(has_high)
        def _():
            halo_copy(q, 0, cell + 1).start()

    def done(q, count):
        pltpu.make_async_copy(sum_of(count), sum_of(count), done_sem.at[q]).wait()

    def finish(q, count):
        done(q, count)

        @pl.loop(0, width)
        def _(where):
            for c in range(2):
                for w in range(local):
                    place_of = (1, c, w, where, *spot(q))
                    pol[place_of] = (pol[place_of].astype(F32) + low[q, where, c, w].astype(F32)).astype(BF16)

        halo(q)

    @pl.when(jnp.logical_not(has_low))
    def _():
        pol[0] = jnp.zeros_like(pol[0])

    @pl.when(jnp.logical_not(has_high))
    def _():
        pol[2] = jnp.zeros_like(pol[2])

    @pl.when(quarter == 0)
    def _():
        @pl.loop(0, chunks + SHIFT)
        def _(t):
            @pl.when(t < chunks)
            def _():
                if width > 1:
                    arrived(0, t, width - 1)
                forward_others(GREATER, t)

            @pl.when(t + ahead < chunks)
            def _():
                forward_own(GREATER, t + ahead)

            @pl.when(t >= SHIFT)
            def _():
                q = t - SHIFT
                forward_own(LESSER, q)
                if width > 1:
                    arrived(1, q, width - 1)
                forward_others(LESSER, q)

        @pl.loop(0, chunks)
        def _(q):
            finish(q, 2 * width)

    @pl.when(quarter == 1)
    def _():
        @pl.loop(0, chunks + SHIFT + LOW_LAG + DONE_LAG)
        def _(t):
            @pl.when(t < chunks)
            def _():
                if width > 1:
                    arrived(0, t, width - 1)

                @pl.when(t >= straight)
                def _():
                    forward_others(GREATER, t)

                arrived(2, t, width)
                lower = recv.at[t, n + 1:n + 1 + width]
                pltpu.make_async_remote_copy(
                    src_ref=lower, dst_ref=lower, send_sem=sent_sem.at[batch(t)], recv_sem=arrive_sem.at[0, t],
                    device_id={"energy": 2 * width + place}, device_id_type=MESH,
                ).start()
                more(t)

            @pl.when(t + ahead < chunks)
            def _():
                forward_own(GREATER, t + ahead)

            late = SHIFT + LOW_LAG

            @pl.when(jnp.logical_and(t >= late, t < chunks + late))
            def _():
                q = t - late
                arrived(1, q, 2 * width - 1)

                @pl.loop(0, half)
                def _(b):
                    correlate(q, b, 0, half - b)

                    @pl.when(b != me)
                    def _():
                        low_copy(q, b).start()

                    @pl.when(b == me)
                    def _():
                        low[q, place] = send_p[q, b]

            @pl.when(t >= late + DONE_LAG)
            def _():
                finish(t - late - DONE_LAG, 2 * width - 1)

    @pl.when(quarter == 2)
    def _():
        @pl.loop(0, chunks + LATE)
        def _(t):
            @pl.when(t < chunks)
            def _():
                arrived(0, t, 6 * width - 2)
                more(t)

                @pl.loop(0, n)
                def _(b):
                    correlate(t, b, jnp.maximum(half - 1 - b, 0), n - b)

                    @pl.when(b != me)
                    def _():
                        return_copy(t, b).start()

                    @pl.when(b == me)
                    def _():
                        pol[1, :, :, place, *spot(t)] = send_p[t, b]

            @pl.when(t >= LATE)
            def _():
                if width > 1:
                    done(t - LATE, width - 1)
                halo(t - LATE)

    @pl.when(quarter == 3)
    def _():
        @pl.loop(straight, chunks)
        def _(t):
            for kind in (GREATER, LESSER):
                if width > 1:
                    arrived(0 if kind == GREATER else 1, t, width - 1)
                forward_others(kind, t)

            @pl.when(t + ahead - straight < chunks)
            def _():
                forward_own(GREATER, t + ahead - straight)
                forward_own(LESSER, t + ahead - straight)

        @pl.loop(0, chunks)
        def _(q):
            done(q, width)
            halo(q)

    coulomb_load.wait()

    def polarized(slot, e, part):
        cols = slice(part * LANES, (part + 1) * LANES)
        return jnp.concatenate([pol[slot, c, e, :, :, cols].reshape(norb, LANES) for c in range(2)], 1)

    last = col_parts - 1

    @pl.loop(0, local)
    def _(e):
        total[e] = nn(coulomb[1], polarized(1, e, last))

    for part in range(col_parts):
        cols = slice(part * LANES, (part + 1) * LANES)
        group = (slice(None), slice(None), slice(None), slice(None), cols)

        @pl.when(has_low)
        def _():
            pltpu.make_async_copy(pol.at[0, *group], pol.at[0, *group], halo_recv_sem.at[0, part]).wait()

        @pl.when(has_high)
        def _():
            pltpu.make_async_copy(pol.at[2, *group], pol.at[2, *group], halo_recv_sem.at[1, part]).wait()

        @pl.loop(0, local)
        def _(e):
            middle = total[e] if part == last else nn(coulomb[1], polarized(1, e, part))
            summed = nn(coulomb[0], polarized(0, e, part)) + nn(coulomb[2], polarized(2, e, part)) + middle
            for c in range(2):
                out[c, e, :, cols] = summed[:, c * LANES:(c + 1) * LANES].astype(BF16)

    @pl.when(has_low)
    def _():
        pltpu.make_async_copy(pol.at[1], pol.at[1], halo_send_sem.at[1]).wait()

    @pl.when(has_high)
    def _():
        pltpu.make_async_copy(pol.at[1], pol.at[1], halo_send_sem.at[0]).wait()

    def all_sent(*counts):
        for i, (count, size) in enumerate(zip(counts, (straight, chunks - straight))):
            if count * size:
                sent = recv.at[0:size, 0:count]
                pltpu.make_async_copy(sent, sent, sent_sem.at[i]).wait()

    @pl.when(quarter == 0)
    def _():
        all_sent(4 * width - 2, 4 * width - 2)

    @pl.when(quarter == 3)
    def _():
        all_sent(2 * width, 4 * width - 2)

    @pl.when(jnp.logical_or(quarter == 1, quarter == 2))
    def _():
        all_sent(6 * width - 3, 6 * width - 3)


def fused(n, cells, retarded, sigma_lesser, sigma_greater, coulomb):
    green = retarded[0]
    local, norb = green.shape[1], green.shape[2]
    width = n // QUARTERS
    strip = norb // width
    chunks = strip // ROWS * (norb // LANES)
    dma = pltpu.SemaphoreType.DMA
    result = pl.pallas_call(
        functools.partial(fused_kernel, n, cells),
        out_shape=pltpu.VMEM(green.shape, BF16),
        in_specs=[pl.BlockSpec(memory_space=pltpu.HBM)] * 4,
        out_specs=pl.BlockSpec(memory_space=pltpu.VMEM),
        scratch_shapes=[
            pltpu.VMEM(green.shape, BF16),
            pltpu.VMEM(green.shape, BF16),
            pltpu.VMEM(green.shape, BF16),
            pltpu.VMEM(coulomb.shape[1:], BF16),
            pltpu.VMEM((2, chunks, width, 2, local, ROWS, LANES), BF16),
            pltpu.VMEM((chunks, 2 * n + 1, 2, local, ROWS, LANES), BF16),
            pltpu.VMEM((chunks, n, 2, local, ROWS, LANES), BF16),
            pltpu.VMEM((chunks, width, 2, local, ROWS, LANES), BF16),
            pltpu.VMEM((3, 2, local, width, strip, norb), BF16),
            pltpu.VMEM((local, norb, 2 * LANES), F32),
            dma((3, local)), dma,
            dma((2,)), dma((3, chunks)), dma((chunks,)),
            dma((2,)), dma((2, norb // LANES)),
        ],
        compiler_params=pltpu.CompilerParams(
            collective_id=0, has_side_effects=True, vmem_limit_bytes=56 * 1024 * 1024
        ),
    )(green, sigma_lesser[0], sigma_greater[0], coulomb[0])
    return result[None]


def thin(n, cells, retarded, sigma_lesser, sigma_greater, coulomb):
    green = retarded[0]
    local = green.shape[1]

    def halves(sigma):
        def product(x, y):
            return jnp.einsum("eik,ekj->eij", x, y, preferred_element_type=F32)

        re = product(green[0], sigma[0]) - product(green[1], sigma[1])
        im = product(green[0], sigma[1]) + product(green[1], sigma[0])
        return re.astype(BF16), im.astype(BF16)

    def adjoint(x, y):
        return jnp.einsum("eik,ejk->eij", x, y, preferred_element_type=F32)

    re, im = halves(sigma_lesser[0])
    lesser = jnp.stack([adjoint(re, green[0]) + adjoint(im, green[1]), adjoint(im, green[0]) - adjoint(re, green[1])])
    re, im = halves(sigma_greater[0])
    greater = jnp.stack([adjoint(green[0], re) + adjoint(green[1], im), adjoint(green[0], im) - adjoint(green[1], re)])
    first = lax.all_to_all(lesser.astype(BF16), "energy", split_axis=2, concat_axis=1, tiled=True).astype(F32)
    second = lax.all_to_all(greater.astype(BF16), "energy", split_axis=2, concat_axis=1, tiled=True).astype(F32)
    energies = n * local
    padded = jnp.concatenate([first, jnp.zeros_like(first)], axis=1)

    def lag(w):
        y = lax.dynamic_slice_in_dim(padded, w, energies, axis=1)
        re = jnp.sum(y[0] * second[0] - y[1] * second[1], axis=0)
        im = jnp.sum(y[0] * second[1] + y[1] * second[0], axis=0)
        return (jnp.stack([re, im]) / math.sqrt(energies)).astype(BF16)

    polarized = jnp.swapaxes(lax.map(lag, jnp.arange(energies)), 0, 1)
    polarized = lax.all_to_all(polarized, "energy", split_axis=1, concat_axis=2, tiled=True)
    up = [(i, i + 1) for i in range(cells - 1)]
    low = lax.ppermute(polarized, "cell", up)
    high = lax.ppermute(polarized, "cell", [(t, s) for s, t in up])
    stacked = jnp.stack([low, polarized, high])
    summed = jnp.einsum("dik,dcekj->ceij", coulomb[0], stacked, preferred_element_type=F32)
    return summed.astype(BF16)[None]


def solution(mesh):
    n, cells = mesh.shape["energy"], mesh.shape["cell"]

    def on_device(retarded, sigma_lesser, sigma_greater, coulomb):
        norb = retarded.shape[-1]
        whole_tiles = n % QUARTERS == 0 and norb % LANES == 0 and norb % (n // QUARTERS * ROWS) == 0
        plan = fused if whole_tiles else thin
        return plan(n, cells, retarded, sigma_lesser, sigma_greater, coulomb)

    in_specs = (
        P("cell", None, "energy", None, None),
        P("cell", None, "energy", None, None),
        P("cell", None, "energy", None, None),
        P("cell", None, None, None),
    )
    out_specs = P("cell", None, "energy", None, None)
    return jax.shard_map(
        on_device, mesh=mesh, in_specs=in_specs, out_specs=out_specs, check_vma=False
    )
```

```python
import functools
import math

import jax
import jax.numpy as jnp
from jax import lax
from jax.experimental import pallas as pl
from jax.experimental.pallas import tpu as pltpu
from jax.sharding import PartitionSpec as P

MESH = pl.DeviceIdType.MESH
ROWS = 16
LANES = 128
QUARTERS = 4
LESSER, GREATER = 0, 1
DIRECT = 1
AHEAD = 3
AHEAD_TOP = 2
EARLY = 4
SHIFT = 1
LOW_LAG = 0
DONE_LAG = 6
LATE = 3
F32 = jnp.float32
BF16 = jnp.bfloat16


def nn(a, b):
    return jnp.dot(a, b, preferred_element_type=F32)


def nt(a, b):
    return lax.dot_general(a, b, (((1,), (1,)), ((), ())), preferred_element_type=F32)


def fused_kernel(
    n, cells, green_in, sig_l_in, sig_g_in, coulomb_in, out,
    green, sig_l, sig_g, coulomb, send, recv, send_p, low, pol, total,
    in_sem, coulomb_sem, sent_sem, arrive_sem, done_sem, halo_send_sem, halo_recv_sem,
):
    me = lax.axis_index("energy")
    cell = lax.axis_index("cell")
    local = green.shape[1]
    norb = green.shape[2]
    width = n // QUARTERS
    half = 2 * width
    quarter, place = me // width, lax.rem(me, width)
    home = jnp.where(quarter == 0, 1, 2)
    strip = norb // width
    row_parts = strip // ROWS
    col_parts = norb // LANES
    chunks = row_parts * col_parts
    straight = min(DIRECT, chunks)
    has_low = cell > 0
    has_high = cell < cells - 1
    offset = {LESSER: 0, GREATER: n + 1}

    def batch(q):
        return jnp.where(q < straight, 0, 1)

    def load(i, e):
        source, held = ((green_in, green), (sig_g_in, sig_g), (sig_l_in, sig_l))[i]
        return pltpu.make_async_copy(source.at[:, e], held.at[:, e], in_sem.at[i, e])

    for e in range(local):
        load(0, e).start()
        load(1, e).start()

    barrier = pltpu.get_barrier_semaphore()

    def greet(other):
        pl.semaphore_signal(barrier, inc=1, device_id={"energy": other}, device_id_type=MESH)

    @pl.loop(1, width)
    def _(k):
        greet(quarter * width + lax.rem(place + k, width))

    def greet_quarter(other):
        @pl.loop(0, width)
        def _(k):
            greet(other * width + k)

    for mine, others in ((0, (1, 2)), (1, (0, 2)), (2, (1, 3)), (3, (2,))):
        @pl.when(quarter == mine)
        def _():
            for other in others:
                greet_quarter(other)

    @pl.when(has_low)
    def _():
        pl.semaphore_signal(barrier, inc=1, device_id={"cell": cell - 1}, device_id_type=MESH)

    @pl.when(has_high)
    def _():
        pl.semaphore_signal(barrier, inc=1, device_id={"cell": cell + 1}, device_id_type=MESH)

    for e in range(local):
        load(2, e).start()
    coulomb_load = pltpu.make_async_copy(coulomb_in, coulomb, coulomb_sem)
    coulomb_load.start()

    def put(value, kind, comp, e):
        value = value.astype(BF16).reshape(width, strip, norb)
        for q in range(chunks):
            c, r = divmod(q, row_parts)
            send[kind, q, :, comp, e] = value[:, r * ROWS:(r + 1) * ROWS, c * LANES:(c + 1) * LANES]

    reach = width * jnp.where(quarter == 1, 2, jnp.where(quarter == 2, 3, 1))

    def meet():
        pl.semaphore_wait(barrier, width - 1 + reach + has_low.astype(jnp.int32) + has_high.astype(jnp.int32))

    pl.when(quarter == 3)(meet)

    def sum_of(count):
        return recv.at[0, 0:count]

    def block_copy(source, kind, q, slot, other, lane):
        return pltpu.make_async_remote_copy(
            src_ref=source, dst_ref=recv.at[q, offset[kind] + slot],
            send_sem=sent_sem.at[batch(q)], recv_sem=arrive_sem.at[lane, q],
            device_id={"energy": other}, device_id_type=MESH,
        )

    @pl.loop(0, local)
    def _(e):
        load(0, e).wait()
        load(1, e).wait()
        g_re, g_im = green[0, e], green[1, e]
        s_re, s_im = sig_g[0, e], sig_g[1, e]
        g_neg = -g_im
        half_re = (nn(g_re, s_re) + nn(g_neg, s_im)).astype(BF16)
        half_im = (nn(g_re, s_im) + nn(g_im, s_re)).astype(BF16)
        put(nt(g_re, half_re) + nt(g_im, half_im), GREATER, 0, e)
        put(nt(g_re, half_im) + nt(g_neg, half_re), GREATER, 1, e)

        @pl.when(quarter == 3)
        def _():
            for q in range(straight):
                @pl.loop(0, width)
                def _(where):
                    pltpu.make_async_remote_copy(
                        src_ref=send.at[GREATER, q, where, :, e], dst_ref=recv.at[q, offset[GREATER] + me, :, e],
                        send_sem=sent_sem.at[batch(q)], recv_sem=arrive_sem.at[0, q],
                        device_id={"energy": home * width + where}, device_id_type=MESH,
                    ).start()

    pl.when(quarter != 3)(meet)


    def exchange(kind, q):
        lane = jnp.where(quarter == 2, 0, 0 if kind == GREATER else 1)

        @pl.loop(1, width)
        def _(k):
            where = lax.rem(place + k, width)
            block_copy(send.at[kind, q, where], kind, q, me, quarter * width + where, lane).start()

    def lane_at_home(kind):
        return jnp.where(quarter == 0, 2 if kind == GREATER else 1, 0)

    def forward_own(kind, q):
        block_copy(send.at[kind, q, place], kind, q, me, home * width + place, lane_at_home(kind)).start()

    def forward_others(kind, q):
        @pl.loop(1, width)
        def _(k):
            slot = quarter * width + lax.rem(place + k, width)
            block_copy(recv.at[q, offset[kind] + slot], kind, q, slot, home * width + place, lane_at_home(kind)).start()

    def arrived(lane, q, count):
        pltpu.make_async_copy(sum_of(count), sum_of(count), arrive_sem.at[lane, q]).wait()

    def direct(kind, q):
        @pl.loop(0, width)
        def _(where):
            block_copy(send.at[kind, q, where], kind, q, me, home * width + where, lane_at_home(kind)).start()

    ahead = jnp.where(quarter == 3, min(AHEAD_TOP, chunks), min(AHEAD, chunks))
    first = jnp.where(quarter == 3, straight, 0)

    @pl.when(quarter == 1)
    def _():
        @pl.loop(0, straight)
        def _(q):
            direct(GREATER, q)

    @pl.when(quarter != 2)
    def _():
        @pl.loop(jnp.where(quarter == 0, 0, straight), ahead)
        def _(q):
            forward_own(GREATER, q)

    @pl.loop(first, ahead)
    def _(q):
        exchange(GREATER, q)

    @pl.loop(0, local)
    def _(e):
        load(2, e).wait()
        g_re, g_im = green[0, e], green[1, e]
        l_re, l_im = sig_l[0, e], sig_l[1, e]
        g_neg = -g_im
        half_re = (nn(g_re, l_re) + nn(g_neg, l_im)).astype(BF16)
        half_im = (nn(g_re, l_im) + nn(g_im, l_re)).astype(BF16)
        put(nt(half_re, g_re) + nt(half_im, g_im), LESSER, 0, e)
        put(nt(half_im, g_re) + nt(half_re, g_neg), LESSER, 1, e)

    @pl.when(quarter == 3)
    def _():
        @pl.loop(0, straight)
        def _(q):
            direct(LESSER, q)

        @pl.loop(straight, ahead)
        def _(q):
            forward_own(LESSER, q)

    @pl.loop(first, ahead)
    def _(q):
        exchange(LESSER, q)

    @pl.loop(ahead, jnp.where(jnp.logical_or(quarter == 1, quarter == 2), min(EARLY, chunks), chunks))
    def _(q):
        exchange(GREATER, q)
        exchange(LESSER, q)

    def more(t):
        @pl.when(t + EARLY < chunks)
        def _():
            exchange(GREATER, t + EARLY)
            exchange(LESSER, t + EARLY)

    blank = jnp.zeros((2, local, ROWS, LANES), BF16)

    @pl.when(jnp.logical_or(quarter == 1, quarter == 2))
    def _():
        @pl.loop(0, chunks)
        def _(q):
            for kind in (LESSER, GREATER):
                recv[q, offset[kind] + me] = send[kind, q, place]

    @pl.when(quarter == 1)
    def _():
        @pl.loop(0, chunks)
        def _(q):
            recv[q, half] = blank

    @pl.when(quarter == 2)
    def _():
        @pl.loop(0, chunks)
        def _(q):
            recv[q, half - 1] = blank
            recv[q, n] = blank

    def spot(q):
        rows = pl.ds(pl.multiple_of(lax.rem(q, row_parts) * ROWS, ROWS), ROWS)
        return rows, pl.ds(pl.multiple_of(q // row_parts * LANES, LANES), LANES)

    def return_copy(q, owner):
        return pltpu.make_async_remote_copy(
            src_ref=send_p.at[q, owner], dst_ref=pol.at[1, :, :, place, *spot(q)],
            send_sem=sent_sem.at[batch(q)], recv_sem=done_sem.at[q],
            device_id={"energy": owner}, device_id_type=MESH,
        )

    def low_copy(q, owner):
        return pltpu.make_async_remote_copy(
            src_ref=send_p.at[q, owner], dst_ref=low.at[q, place],
            send_sem=sent_sem.at[batch(q)], recv_sem=done_sem.at[q],
            device_id={"energy": owner}, device_id_type=MESH,
        )

    def halo_copy(q, slot, other):
        return pltpu.make_async_remote_copy(
            src_ref=pol.at[1, :, :, :, *spot(q)], dst_ref=pol.at[slot, :, :, :, *spot(q)],
            send_sem=halo_send_sem.at[slot // 2], recv_sem=halo_recv_sem.at[slot // 2, q // row_parts],
            device_id={"cell": other}, device_id_type=MESH,
        )

    factor = 1.0 / math.sqrt(n * local)

    def correlate(q, b, first_step, last_step):
        def step(a, acc):
            first = [
                (recv[q, a + b + i // local, 0, i % local].astype(F32), recv[q, a + b + i // local, 1, i % local].astype(F32))
                for i in range(2 * local - 1)
            ]
            acc = list(acc)
            for e in range(local):
                x_re, x_im = recv[q, n + 1 + a, 0, e].astype(F32), recv[q, n + 1 + a, 1, e].astype(F32)
                for w in range(local):
                    y_re, y_im = first[e + w]
                    acc[2 * w] = acc[2 * w] + (y_re * x_re - y_im * x_im)
                    acc[2 * w + 1] = acc[2 * w + 1] + (y_re * x_im + y_im * x_re)
            return tuple(acc)

        zero = jnp.zeros((ROWS, LANES), F32)
        acc = lax.fori_loop(first_step, last_step, step, (zero,) * (2 * local))
        for w in range(local):
            send_p[q, b, 0, w] = (acc[2 * w] * factor).astype(BF16)
            send_p[q, b, 1, w] = (acc[2 * w + 1] * factor).astype(BF16)

    def halo(q):
        @pl.when(has_low)
        def _():
            halo_copy(q, 2, cell - 1).start()

        @pl.when(has_high)
        def _():
            halo_copy(q, 0, cell + 1).start()

    def done(q, count):
        pltpu.make_async_copy(sum_of(count), sum_of(count), done_sem.at[q]).wait()

    def finish(q, count):
        done(q, count)

        @pl.loop(0, width)
        def _(where):
            for c in range(2):
                for w in range(local):
                    place_of = (1, c, w, where, *spot(q))
                    pol[place_of] = (pol[place_of].astype(F32) + low[q, where, c, w].astype(F32)).astype(BF16)

        halo(q)

    @pl.when(jnp.logical_not(has_low))
    def _():
        pol[0] = jnp.zeros_like(pol[0])

    @pl.when(jnp.logical_not(has_high))
    def _():
        pol[2] = jnp.zeros_like(pol[2])

    @pl.when(quarter == 0)
    def _():
        @pl.loop(0, chunks + SHIFT)
        def _(t):
            @pl.when(t < chunks)
            def _():
                if width > 1:
                    arrived(0, t, width - 1)
                forward_others(GREATER, t)

            @pl.when(t + ahead < chunks)
            def _():
                forward_own(GREATER, t + ahead)

            @pl.when(t >= SHIFT)
            def _():
                q = t - SHIFT
                forward_own(LESSER, q)
                if width > 1:
                    arrived(1, q, width - 1)
                forward_others(LESSER, q)

        @pl.loop(0, chunks)
        def _(q):
            finish(q, 2 * width)

    @pl.when(quarter == 1)
    def _():
        @pl.loop(0, chunks + SHIFT + LOW_LAG + DONE_LAG)
        def _(t):
            @pl.when(t < chunks)
            def _():
                if width > 1:
                    arrived(0, t, width - 1)

                @pl.when(t >= straight)
                def _():
                    forward_others(GREATER, t)

                arrived(2, t, width)
                lower = recv.at[t, n + 1:n + 1 + width]
                pltpu.make_async_remote_copy(
                    src_ref=lower, dst_ref=lower, send_sem=sent_sem.at[batch(t)], recv_sem=arrive_sem.at[0, t],
                    device_id={"energy": 2 * width + place}, device_id_type=MESH,
                ).start()
                more(t)

            @pl.when(t + ahead < chunks)
            def _():
                forward_own(GREATER, t + ahead)

            late = SHIFT + LOW_LAG

            @pl.when(jnp.logical_and(t >= late, t < chunks + late))
            def _():
                q = t - late
                arrived(1, q, 2 * width - 1)

                @pl.loop(0, half)
                def _(b):
                    correlate(q, b, 0, half - b)

                    @pl.when(b != me)
                    def _():
                        low_copy(q, b).start()

                    @pl.when(b == me)
                    def _():
                        low[q, place] = send_p[q, b]

            @pl.when(t >= late + DONE_LAG)
            def _():
                finish(t - late - DONE_LAG, 2 * width - 1)

    @pl.when(quarter == 2)
    def _():
        @pl.loop(0, chunks + LATE)
        def _(t):
            @pl.when(t < chunks)
            def _():
                arrived(0, t, 6 * width - 2)
                more(t)

                @pl.loop(0, n)
                def _(b):
                    correlate(t, b, jnp.maximum(half - 1 - b, 0), n - b)

                    @pl.when(b != me)
                    def _():
                        return_copy(t, b).start()

                    @pl.when(b == me)
                    def _():
                        pol[1, :, :, place, *spot(t)] = send_p[t, b]

            @pl.when(t >= LATE)
            def _():
                if width > 1:
                    done(t - LATE, width - 1)
                halo(t - LATE)

    @pl.when(quarter == 3)
    def _():
        @pl.loop(straight, chunks)
        def _(t):
            for kind in (GREATER, LESSER):
                if width > 1:
                    arrived(0 if kind == GREATER else 1, t, width - 1)
                forward_others(kind, t)

            @pl.when(t + ahead - straight < chunks)
            def _():
                forward_own(GREATER, t + ahead - straight)
                forward_own(LESSER, t + ahead - straight)

        @pl.loop(0, chunks)
        def _(q):
            done(q, width)
            halo(q)

    coulomb_load.wait()

    def polarized(slot, e, part):
        cols = slice(part * LANES, (part + 1) * LANES)
        return jnp.concatenate([pol[slot, c, e, :, :, cols].reshape(norb, LANES) for c in range(2)], 1)

    last = col_parts - 1

    @pl.loop(0, local)
    def _(e):
        total[e] = nn(coulomb[1], polarized(1, e, last))

    for part in range(col_parts):
        cols = slice(part * LANES, (part + 1) * LANES)
        group = (slice(None), slice(None), slice(None), slice(None), cols)

        @pl.when(has_low)
        def _():
            pltpu.make_async_copy(pol.at[0, *group], pol.at[0, *group], halo_recv_sem.at[0, part]).wait()

        @pl.when(has_high)
        def _():
            pltpu.make_async_copy(pol.at[2, *group], pol.at[2, *group], halo_recv_sem.at[1, part]).wait()

        @pl.loop(0, local)
        def _(e):
            middle = total[e] if part == last else nn(coulomb[1], polarized(1, e, part))
            summed = nn(coulomb[0], polarized(0, e, part)) + nn(coulomb[2], polarized(2, e, part)) + middle
            for c in range(2):
                out[c, e, :, cols] = summed[:, c * LANES:(c + 1) * LANES].astype(BF16)

    @pl.when(has_low)
    def _():
        pltpu.make_async_copy(pol.at[1], pol.at[1], halo_send_sem.at[1]).wait()

    @pl.when(has_high)
    def _():
        pltpu.make_async_copy(pol.at[1], pol.at[1], halo_send_sem.at[0]).wait()

    def all_sent(*counts):
        for i, (count, size) in enumerate(zip(counts, (straight, chunks - straight))):
            if count * size:
                sent = recv.at[0:size, 0:count]
                pltpu.make_async_copy(sent, sent, sent_sem.at[i]).wait()

    @pl.when(quarter == 0)
    def _():
        all_sent(4 * width - 2, 4 * width - 2)

    @pl.when(quarter == 3)
    def _():
        all_sent(2 * width, 4 * width - 2)

    @pl.when(jnp.logical_or(quarter == 1, quarter == 2))
    def _():
        all_sent(6 * width - 3, 6 * width - 3)


def fused(n, cells, retarded, sigma_lesser, sigma_greater, coulomb):
    green = retarded[0]
    local, norb = green.shape[1], green.shape[2]
    width = n // QUARTERS
    strip = norb // width
    chunks = strip // ROWS * (norb // LANES)
    dma = pltpu.SemaphoreType.DMA
    result = pl.pallas_call(
        functools.partial(fused_kernel, n, cells),
        out_shape=pltpu.VMEM(green.shape, BF16),
        in_specs=[pl.BlockSpec(memory_space=pltpu.HBM)] * 4,
        out_specs=pl.BlockSpec(memory_space=pltpu.VMEM),
        scratch_shapes=[
            pltpu.VMEM(green.shape, BF16),
            pltpu.VMEM(green.shape, BF16),
            pltpu.VMEM(green.shape, BF16),
            pltpu.VMEM(coulomb.shape[1:], BF16),
            pltpu.VMEM((2, chunks, width, 2, local, ROWS, LANES), BF16),
            pltpu.VMEM((chunks, 2 * n + 1, 2, local, ROWS, LANES), BF16),
            pltpu.VMEM((chunks, n, 2, local, ROWS, LANES), BF16),
            pltpu.VMEM((chunks, width, 2, local, ROWS, LANES), BF16),
            pltpu.VMEM((3, 2, local, width, strip, norb), BF16),
            pltpu.VMEM((local, norb, 2 * LANES), F32),
            dma((3, local)), dma,
            dma((2,)), dma((3, chunks)), dma((chunks,)),
            dma((2,)), dma((2, norb // LANES)),
        ],
        compiler_params=pltpu.CompilerParams(
            collective_id=0, has_side_effects=True, vmem_limit_bytes=56 * 1024 * 1024
        ),
    )(green, sigma_lesser[0], sigma_greater[0], coulomb[0])
    return result[None]


def thin(n, cells, retarded, sigma_lesser, sigma_greater, coulomb):
    green = retarded[0]
    local = green.shape[1]

    def halves(sigma):
        def product(x, y):
            return jnp.einsum("eik,ekj->eij", x, y, preferred_element_type=F32)

        re = product(green[0], sigma[0]) - product(green[1], sigma[1])
        im = product(green[0], sigma[1]) + product(green[1], sigma[0])
        return re.astype(BF16), im.astype(BF16)

    def adjoint(x, y):
        return jnp.einsum("eik,ejk->eij", x, y, preferred_element_type=F32)

    re, im = halves(sigma_lesser[0])
    lesser = jnp.stack([adjoint(re, green[0]) + adjoint(im, green[1]), adjoint(im, green[0]) - adjoint(re, green[1])])
    re, im = halves(sigma_greater[0])
    greater = jnp.stack([adjoint(green[0], re) + adjoint(green[1], im), adjoint(green[0], im) - adjoint(green[1], re)])
    first = lax.all_to_all(lesser.astype(BF16), "energy", split_axis=2, concat_axis=1, tiled=True).astype(F32)
    second = lax.all_to_all(greater.astype(BF16), "energy", split_axis=2, concat_axis=1, tiled=True).astype(F32)
    energies = n * local
    padded = jnp.concatenate([first, jnp.zeros_like(first)], axis=1)

    def lag(w):
        y = lax.dynamic_slice_in_dim(padded, w, energies, axis=1)
        re = jnp.sum(y[0] * second[0] - y[1] * second[1], axis=0)
        im = jnp.sum(y[0] * second[1] + y[1] * second[0], axis=0)
        return (jnp.stack([re, im]) / math.sqrt(energies)).astype(BF16)

    polarized = jnp.swapaxes(lax.map(lag, jnp.arange(energies)), 0, 1)
    polarized = lax.all_to_all(polarized, "energy", split_axis=1, concat_axis=2, tiled=True)
    up = [(i, i + 1) for i in range(cells - 1)]
    low = lax.ppermute(polarized, "cell", up)
    high = lax.ppermute(polarized, "cell", [(t, s) for s, t in up])
    stacked = jnp.stack([low, polarized, high])
    summed = jnp.einsum("dik,dcekj->ceij", coulomb[0], stacked, preferred_element_type=F32)
    return summed.astype(BF16)[None]


def solution(mesh):
    n, cells = mesh.shape["energy"], mesh.shape["cell"]

    def on_device(retarded, sigma_lesser, sigma_greater, coulomb):
        norb = retarded.shape[-1]
        whole_tiles = n % QUARTERS == 0 and norb % LANES == 0 and norb % (n // QUARTERS * ROWS) == 0
        plan = fused if whole_tiles else thin
        return plan(n, cells, retarded, sigma_lesser, sigma_greater, coulomb)

    in_specs = (
        P("cell", None, "energy", None, None),
        P("cell", None, "energy", None, None),
        P("cell", None, "energy", None, None),
        P("cell", None, None, None),
    )
    out_specs = P("cell", None, "energy", None, None)
    return jax.shard_map(
        on_device, mesh=mesh, in_specs=in_specs, out_specs=out_specs, check_vma=False
    )
```

```python
import functools
import math

import jax
import jax.numpy as jnp
from jax import lax
from jax.experimental import pallas as pl
from jax.experimental.pallas import tpu as pltpu
from jax.sharding import PartitionSpec as P

MESH = pl.DeviceIdType.MESH
ROWS = 16
LANES = 128
QUARTERS = 4
LESSER, GREATER = 0, 1
DIRECT = 1
AHEAD = 3
AHEAD_TOP = 2
EARLY = 4
LOW_LAG = 8
DONE_LAG = 6
LATE = 3
F32 = jnp.float32
BF16 = jnp.bfloat16


def nn(a, b):
    return jnp.dot(a, b, preferred_element_type=F32)


def nt(a, b):
    return lax.dot_general(a, b, (((1,), (1,)), ((), ())), preferred_element_type=F32)


def fused_kernel(
    n, cells, green_in, sig_l_in, sig_g_in, coulomb_in, out,
    green, sig_l, sig_g, coulomb, send, recv, send_p, low, part, pol, total,
    in_sem, coulomb_sem, sent_sem, arrive_sem, done_sem, halo_send_sem, halo_recv_sem,
):
    me = lax.axis_index("energy")
    cell = lax.axis_index("cell")
    local = green.shape[1]
    norb = green.shape[2]
    width = n // QUARTERS
    half = 2 * width
    quarter, place = me // width, lax.rem(me, width)
    home = jnp.where(quarter == 0, 1, 2)
    strip = norb // width
    row_parts = strip // ROWS
    col_parts = norb // LANES
    chunks = row_parts * col_parts
    straight = min(DIRECT, chunks)
    has_low = cell > 0
    has_high = cell < cells - 1
    offset = {LESSER: 0, GREATER: n + 1}

    def batch(q):
        return jnp.where(q < straight, 0, 1)

    def load(i, e):
        source, held = ((green_in, green), (sig_g_in, sig_g), (sig_l_in, sig_l))[i]
        return pltpu.make_async_copy(source.at[:, e], held.at[:, e], in_sem.at[i, e])

    for e in range(local):
        load(0, e).start()
        load(1, e).start()

    barrier = pltpu.get_barrier_semaphore()

    def greet(other):
        pl.semaphore_signal(barrier, inc=1, device_id={"energy": other}, device_id_type=MESH)

    @pl.loop(1, width)
    def _(k):
        greet(quarter * width + lax.rem(place + k, width))

    def greet_quarter(other):
        @pl.loop(0, width)
        def _(k):
            greet(other * width + k)

    for mine, others in ((0, (1, 2)), (1, (0, 2)), (2, (1, 3)), (3, (2,))):
        @pl.when(quarter == mine)
        def _():
            for other in others:
                greet_quarter(other)

    @pl.when(has_low)
    def _():
        pl.semaphore_signal(barrier, inc=1, device_id={"cell": cell - 1}, device_id_type=MESH)

    @pl.when(has_high)
    def _():
        pl.semaphore_signal(barrier, inc=1, device_id={"cell": cell + 1}, device_id_type=MESH)

    for e in range(local):
        load(2, e).start()
    coulomb_load = pltpu.make_async_copy(coulomb_in, coulomb, coulomb_sem)
    coulomb_load.start()

    def put(value, kind, comp, e):
        value = value.astype(BF16).reshape(width, strip, norb)
        for q in range(chunks):
            c, r = divmod(q, row_parts)
            send[kind, q, :, comp, e] = value[:, r * ROWS:(r + 1) * ROWS, c * LANES:(c + 1) * LANES]

    reach = width * jnp.where(quarter == 1, 2, jnp.where(quarter == 2, 3, 1))

    def meet():
        pl.semaphore_wait(barrier, width - 1 + reach + has_low.astype(jnp.int32) + has_high.astype(jnp.int32))

    pl.when(quarter == 3)(meet)

    def sum_of(count):
        return recv.at[0, 0:count]

    def block_copy(source, kind, q, slot, other, lane):
        return pltpu.make_async_remote_copy(
            src_ref=source, dst_ref=recv.at[q, offset[kind] + slot],
            send_sem=sent_sem.at[batch(q)], recv_sem=arrive_sem.at[lane, q],
            device_id={"energy": other}, device_id_type=MESH,
        )

    @pl.loop(0, local)
    def _(e):
        load(0, e).wait()
        load(1, e).wait()
        g_re, g_im = green[0, e], green[1, e]
        s_re, s_im = sig_g[0, e], sig_g[1, e]
        g_neg = -g_im
        half_re = (nn(g_re, s_re) + nn(g_neg, s_im)).astype(BF16)
        half_im = (nn(g_re, s_im) + nn(g_im, s_re)).astype(BF16)
        put(nt(g_re, half_re) + nt(g_im, half_im), GREATER, 0, e)
        put(nt(g_re, half_im) + nt(g_neg, half_re), GREATER, 1, e)

        @pl.when(quarter == 3)
        def _():
            for q in range(straight):
                @pl.loop(0, width)
                def _(where):
                    pltpu.make_async_remote_copy(
                        src_ref=send.at[GREATER, q, where, :, e], dst_ref=recv.at[q, offset[GREATER] + me, :, e],
                        send_sem=sent_sem.at[batch(q)], recv_sem=arrive_sem.at[0, q],
                        device_id={"energy": home * width + where}, device_id_type=MESH,
                    ).start()

    pl.when(quarter != 3)(meet)


    def exchange(kind, q):
        lane = jnp.where(quarter == 2, 0, 0 if kind == GREATER else 1)

        @pl.loop(1, width)
        def _(k):
            where = lax.rem(place + k, width)
            block_copy(send.at[kind, q, where], kind, q, me, quarter * width + where, lane).start()

    def lane_at_home(kind):
        return jnp.where(quarter == 0, 2 if kind == GREATER else 1, 0)

    def forward_own(kind, q):
        block_copy(send.at[kind, q, place], kind, q, me, home * width + place, lane_at_home(kind)).start()

    def forward_others(kind, q):
        @pl.loop(1, width)
        def _(k):
            slot = quarter * width + lax.rem(place + k, width)
            block_copy(recv.at[q, offset[kind] + slot], kind, q, slot, home * width + place, lane_at_home(kind)).start()

    def arrived(lane, q, count):
        pltpu.make_async_copy(sum_of(count), sum_of(count), arrive_sem.at[lane, q]).wait()

    def direct(kind, q):
        @pl.loop(0, width)
        def _(where):
            block_copy(send.at[kind, q, where], kind, q, me, home * width + where, lane_at_home(kind)).start()

    ahead = jnp.where(quarter == 3, min(AHEAD_TOP, chunks), min(AHEAD, chunks))
    first = jnp.where(quarter == 3, straight, 0)

    @pl.when(quarter == 1)
    def _():
        @pl.loop(0, straight)
        def _(q):
            direct(GREATER, q)

    @pl.when(quarter != 2)
    def _():
        @pl.loop(jnp.where(quarter == 0, 0, straight), ahead)
        def _(q):
            forward_own(GREATER, q)

    @pl.loop(first, ahead)
    def _(q):
        exchange(GREATER, q)

    @pl.loop(0, local)
    def _(e):
        load(2, e).wait()
        g_re, g_im = green[0, e], green[1, e]
        l_re, l_im = sig_l[0, e], sig_l[1, e]
        g_neg = -g_im
        half_re = (nn(g_re, l_re) + nn(g_neg, l_im)).astype(BF16)
        half_im = (nn(g_re, l_im) + nn(g_im, l_re)).astype(BF16)
        put(nt(half_re, g_re) + nt(half_im, g_im), LESSER, 0, e)
        put(nt(half_im, g_re) + nt(half_re, g_neg), LESSER, 1, e)

    @pl.when(quarter == 3)
    def _():
        @pl.loop(0, straight)
        def _(q):
            direct(LESSER, q)

        @pl.loop(straight, ahead)
        def _(q):
            forward_own(LESSER, q)

    @pl.loop(first, ahead)
    def _(q):
        exchange(LESSER, q)

    @pl.loop(ahead, jnp.where(jnp.logical_or(quarter == 1, quarter == 2), min(EARLY, chunks), chunks))
    def _(q):
        exchange(GREATER, q)
        exchange(LESSER, q)

    def more(t):
        @pl.when(t + EARLY < chunks)
        def _():
            exchange(GREATER, t + EARLY)
            exchange(LESSER, t + EARLY)

    blank = jnp.zeros((2, local, ROWS, LANES), BF16)

    @pl.when(quarter != 3)
    def _():
        @pl.loop(0, chunks)
        def _(q):
            for kind in (LESSER, GREATER):
                recv[q, offset[kind] + me] = send[kind, q, place]

    @pl.when(quarter == 1)
    def _():
        @pl.loop(0, chunks)
        def _(q):
            recv[q, width - 1] = blank
            recv[q, half] = blank

    @pl.when(quarter == 0)
    def _():
        @pl.loop(0, chunks)
        def _(q):
            recv[q, width] = blank

    @pl.when(quarter == 2)
    def _():
        @pl.loop(0, chunks)
        def _(q):
            recv[q, half - 1] = blank
            recv[q, n] = blank

    def spot(q):
        rows = pl.ds(pl.multiple_of(lax.rem(q, row_parts) * ROWS, ROWS), ROWS)
        return rows, pl.ds(pl.multiple_of(q // row_parts * LANES, LANES), LANES)

    def return_copy(q, owner):
        return pltpu.make_async_remote_copy(
            src_ref=send_p.at[q, owner], dst_ref=pol.at[1, :, :, place, *spot(q)],
            send_sem=sent_sem.at[batch(q)], recv_sem=done_sem.at[q],
            device_id={"energy": owner}, device_id_type=MESH,
        )

    def low_copy(q, owner):
        return pltpu.make_async_remote_copy(
            src_ref=send_p.at[q, owner], dst_ref=low.at[q, place],
            send_sem=sent_sem.at[batch(q)], recv_sem=done_sem.at[q],
            device_id={"energy": owner}, device_id_type=MESH,
        )

    def halo_copy(q, slot, other):
        return pltpu.make_async_remote_copy(
            src_ref=pol.at[1, :, :, :, *spot(q)], dst_ref=pol.at[slot, :, :, :, *spot(q)],
            send_sem=halo_send_sem.at[slot // 2], recv_sem=halo_recv_sem.at[slot // 2, q // row_parts],
            device_id={"cell": other}, device_id_type=MESH,
        )

    factor = 1.0 / math.sqrt(n * local)

    def correlate(q, b, first_step, last_step, extra=None):
        def step(a, acc):
            first = [
                (recv[q, a + b + i // local, 0, i % local].astype(F32), recv[q, a + b + i // local, 1, i % local].astype(F32))
                for i in range(2 * local - 1)
            ]
            acc = list(acc)
            for e in range(local):
                x_re, x_im = recv[q, n + 1 + a, 0, e].astype(F32), recv[q, n + 1 + a, 1, e].astype(F32)
                for w in range(local):
                    y_re, y_im = first[e + w]
                    acc[2 * w] = acc[2 * w] + (y_re * x_re - y_im * x_im)
                    acc[2 * w + 1] = acc[2 * w + 1] + (y_re * x_im + y_im * x_re)
            return tuple(acc)

        zero = jnp.zeros((ROWS, LANES), F32)
        acc = lax.fori_loop(first_step, last_step, step, (zero,) * (2 * local))
        for w in range(local):
            for c in range(2):
                value = acc[2 * w + c] * factor
                if extra is not None:
                    value = value + extra[q, b, c, w].astype(F32)
                send_p[q, b, c, w] = value.astype(BF16)

    def halo(q):
        @pl.when(has_low)
        def _():
            halo_copy(q, 2, cell - 1).start()

        @pl.when(has_high)
        def _():
            halo_copy(q, 0, cell + 1).start()

    def done(q, count):
        pltpu.make_async_copy(sum_of(count), sum_of(count), done_sem.at[q]).wait()

    def finish(q, count):
        done(q, count)

        @pl.loop(0, width)
        def _(where):
            for c in range(2):
                for w in range(local):
                    place_of = (1, c, w, where, *spot(q))
                    pol[place_of] = (pol[place_of].astype(F32) + low[q, where, c, w].astype(F32)).astype(BF16)

        halo(q)

    @pl.when(jnp.logical_not(has_low))
    def _():
        pol[0] = jnp.zeros_like(pol[0])

    @pl.when(jnp.logical_not(has_high))
    def _():
        pol[2] = jnp.zeros_like(pol[2])

    def low_out(q, b):
        @pl.when(b != me)
        def _():
            low_copy(q, b).start()

        @pl.when(b == me)
        def _():
            low[q, place] = send_p[q, b]

    def part_copy(q, b):
        return pltpu.make_async_remote_copy(
            src_ref=send_p.at[q, b], dst_ref=part.at[q, b],
            send_sem=sent_sem.at[batch(q)], recv_sem=arrive_sem.at[2, q],
            device_id={"energy": place}, device_id_type=MESH,
        )

    @pl.when(quarter == 0)
    def _():
        @pl.loop(0, chunks)
        def _(t):
            if width > 1:
                arrived(0, t, width - 1)
            forward_others(GREATER, t)

            @pl.when(t + ahead < chunks)
            def _():
                forward_own(GREATER, t + ahead)

        @pl.loop(0, chunks + LOW_LAG)
        def _(t):
            @pl.when(t < chunks)
            def _():
                if width > 1:
                    arrived(1, t, width - 1)
                arrived(2, t, width)

                @pl.loop(0, width)
                def _(b):
                    correlate(t, b, 0, width - b, part)
                    low_out(t, b)

            @pl.when(t >= LOW_LAG)
            def _():
                finish(t - LOW_LAG, 2 * width - 1)

    @pl.when(quarter == 1)
    def _():
        @pl.loop(0, chunks + DONE_LAG)
        def _(t):
            @pl.when(t < chunks)
            def _():
                if width > 1:
                    arrived(0, t, width - 1)

                @pl.when(t >= straight)
                def _():
                    forward_others(GREATER, t)

                arrived(2, t, width)
                lower = recv.at[t, n + 1:n + 1 + width]
                pltpu.make_async_remote_copy(
                    src_ref=lower, dst_ref=lower, send_sem=sent_sem.at[batch(t)], recv_sem=arrive_sem.at[0, t],
                    device_id={"energy": 2 * width + place}, device_id_type=MESH,
                ).start()
                more(t)

            @pl.when(t + ahead < chunks)
            def _():
                forward_own(GREATER, t + ahead)

            @pl.when(t < chunks)
            def _():
                if width > 1:
                    arrived(1, t, width - 1)

                @pl.loop(0, half)
                def _(b):
                    correlate(t, b, jnp.maximum(width - 1 - b, 0), half - b)

                    @pl.when(b < width)
                    def _():
                        part_copy(t, b).start()

                    @pl.when(b >= width)
                    def _():
                        low_out(t, b)

            @pl.when(t >= DONE_LAG)
            def _():
                finish(t - DONE_LAG, 2 * width - 1)

    @pl.when(quarter == 2)
    def _():
        @pl.loop(0, chunks + LATE)
        def _(t):
            @pl.when(t < chunks)
            def _():
                arrived(0, t, 6 * width - 2)
                more(t)

                @pl.loop(0, n)
                def _(b):
                    correlate(t, b, jnp.maximum(half - 1 - b, 0), n - b)

                    @pl.when(b != me)
                    def _():
                        return_copy(t, b).start()

                    @pl.when(b == me)
                    def _():
                        pol[1, :, :, place, *spot(t)] = send_p[t, b]

            @pl.when(t >= LATE)
            def _():
                if width > 1:
                    done(t - LATE, width - 1)
                halo(t - LATE)

    @pl.when(quarter == 3)
    def _():
        @pl.loop(straight, chunks)
        def _(t):
            for kind in (GREATER, LESSER):
                if width > 1:
                    arrived(0 if kind == GREATER else 1, t, width - 1)
                forward_others(kind, t)

            @pl.when(t + ahead - straight < chunks)
            def _():
                forward_own(GREATER, t + ahead - straight)
                forward_own(LESSER, t + ahead - straight)

        @pl.loop(0, chunks)
        def _(q):
            done(q, width)
            halo(q)

    coulomb_load.wait()

    def polarized(slot, e, part):
        cols = slice(part * LANES, (part + 1) * LANES)
        return jnp.concatenate([pol[slot, c, e, :, :, cols].reshape(norb, LANES) for c in range(2)], 1)

    last = col_parts - 1

    @pl.loop(0, local)
    def _(e):
        total[e] = nn(coulomb[1], polarized(1, e, last))

    for part in range(col_parts):
        cols = slice(part * LANES, (part + 1) * LANES)
        group = (slice(None), slice(None), slice(None), slice(None), cols)

        @pl.when(has_low)
        def _():
            pltpu.make_async_copy(pol.at[0, *group], pol.at[0, *group], halo_recv_sem.at[0, part]).wait()

        @pl.when(has_high)
        def _():
            pltpu.make_async_copy(pol.at[2, *group], pol.at[2, *group], halo_recv_sem.at[1, part]).wait()

        @pl.loop(0, local)
        def _(e):
            middle = total[e] if part == last else nn(coulomb[1], polarized(1, e, part))
            summed = nn(coulomb[0], polarized(0, e, part)) + nn(coulomb[2], polarized(2, e, part)) + middle
            for c in range(2):
                out[c, e, :, cols] = summed[:, c * LANES:(c + 1) * LANES].astype(BF16)

    @pl.when(has_low)
    def _():
        pltpu.make_async_copy(pol.at[1], pol.at[1], halo_send_sem.at[1]).wait()

    @pl.when(has_high)
    def _():
        pltpu.make_async_copy(pol.at[1], pol.at[1], halo_send_sem.at[0]).wait()

    def all_sent(*counts):
        for i, (count, size) in enumerate(zip(counts, (straight, chunks - straight))):
            if count * size:
                sent = recv.at[0:size, 0:count]
                pltpu.make_async_copy(sent, sent, sent_sem.at[i]).wait()

    @pl.when(quarter == 0)
    def _():
        all_sent(4 * width - 3, 4 * width - 3)

    @pl.when(quarter == 3)
    def _():
        all_sent(2 * width, 4 * width - 2)

    @pl.when(jnp.logical_or(quarter == 1, quarter == 2))
    def _():
        all_sent(6 * width - 3, 6 * width - 3)


def fused(n, cells, retarded, sigma_lesser, sigma_greater, coulomb):
    green = retarded[0]
    local, norb = green.shape[1], green.shape[2]
    width = n // QUARTERS
    strip = norb // width
    chunks = strip // ROWS * (norb // LANES)
    dma = pltpu.SemaphoreType.DMA
    result = pl.pallas_call(
        functools.partial(fused_kernel, n, cells),
        out_shape=pltpu.VMEM(green.shape, BF16),
        in_specs=[pl.BlockSpec(memory_space=pltpu.HBM)] * 4,
        out_specs=pl.BlockSpec(memory_space=pltpu.VMEM),
        scratch_shapes=[
            pltpu.VMEM(green.shape, BF16),
            pltpu.VMEM(green.shape, BF16),
            pltpu.VMEM(green.shape, BF16),
            pltpu.VMEM(coulomb.shape[1:], BF16),
            pltpu.VMEM((2, chunks, width, 2, local, ROWS, LANES), BF16),
            pltpu.VMEM((chunks, 2 * n + 1, 2, local, ROWS, LANES), BF16),
            pltpu.VMEM((chunks, n, 2, local, ROWS, LANES), BF16),
            pltpu.VMEM((chunks, width, 2, local, ROWS, LANES), BF16),
            pltpu.VMEM((chunks, width, 2, local, ROWS, LANES), BF16),
            pltpu.VMEM((3, 2, local, width, strip, norb), BF16),
            pltpu.VMEM((local, norb, 2 * LANES), F32),
            dma((3, local)), dma,
            dma((2,)), dma((3, chunks)), dma((chunks,)),
            dma((2,)), dma((2, norb // LANES)),
        ],
        compiler_params=pltpu.CompilerParams(
            collective_id=0, has_side_effects=True, vmem_limit_bytes=56 * 1024 * 1024
        ),
    )(green, sigma_lesser[0], sigma_greater[0], coulomb[0])
    return result[None]


def thin(n, cells, retarded, sigma_lesser, sigma_greater, coulomb):
    green = retarded[0]
    local = green.shape[1]

    def halves(sigma):
        def product(x, y):
            return jnp.einsum("eik,ekj->eij", x, y, preferred_element_type=F32)

        re = product(green[0], sigma[0]) - product(green[1], sigma[1])
        im = product(green[0], sigma[1]) + product(green[1], sigma[0])
        return re.astype(BF16), im.astype(BF16)

    def adjoint(x, y):
        return jnp.einsum("eik,ejk->eij", x, y, preferred_element_type=F32)

    re, im = halves(sigma_lesser[0])
    lesser = jnp.stack([adjoint(re, green[0]) + adjoint(im, green[1]), adjoint(im, green[0]) - adjoint(re, green[1])])
    re, im = halves(sigma_greater[0])
    greater = jnp.stack([adjoint(green[0], re) + adjoint(green[1], im), adjoint(green[0], im) - adjoint(green[1], re)])
    first = lax.all_to_all(lesser.astype(BF16), "energy", split_axis=2, concat_axis=1, tiled=True).astype(F32)
    second = lax.all_to_all(greater.astype(BF16), "energy", split_axis=2, concat_axis=1, tiled=True).astype(F32)
    energies = n * local
    padded = jnp.concatenate([first, jnp.zeros_like(first)], axis=1)

    def lag(w):
        y = lax.dynamic_slice_in_dim(padded, w, energies, axis=1)
        re = jnp.sum(y[0] * second[0] - y[1] * second[1], axis=0)
        im = jnp.sum(y[0] * second[1] + y[1] * second[0], axis=0)
        return (jnp.stack([re, im]) / math.sqrt(energies)).astype(BF16)

    polarized = jnp.swapaxes(lax.map(lag, jnp.arange(energies)), 0, 1)
    polarized = lax.all_to_all(polarized, "energy", split_axis=1, concat_axis=2, tiled=True)
    up = [(i, i + 1) for i in range(cells - 1)]
    low = lax.ppermute(polarized, "cell", up)
    high = lax.ppermute(polarized, "cell", [(t, s) for s, t in up])
    stacked = jnp.stack([low, polarized, high])
    summed = jnp.einsum("dik,dcekj->ceij", coulomb[0], stacked, preferred_element_type=F32)
    return summed.astype(BF16)[None]


def solution(mesh):
    n, cells = mesh.shape["energy"], mesh.shape["cell"]

    def on_device(retarded, sigma_lesser, sigma_greater, coulomb):
        norb = retarded.shape[-1]
        whole_tiles = n % QUARTERS == 0 and norb % LANES == 0 and norb % (n // QUARTERS * ROWS) == 0
        plan = fused if whole_tiles else thin
        return plan(n, cells, retarded, sigma_lesser, sigma_greater, coulomb)

    in_specs = (
        P("cell", None, "energy", None, None),
        P("cell", None, "energy", None, None),
        P("cell", None, "energy", None, None),
        P("cell", None, None, None),
    )
    out_specs = P("cell", None, "energy", None, None)
    return jax.shard_map(
        on_device, mesh=mesh, in_specs=in_specs, out_specs=out_specs, check_vma=False
    )
```

```python
import functools
import math

import jax
import jax.numpy as jnp
from jax import lax
from jax.experimental import pallas as pl
from jax.experimental.pallas import tpu as pltpu
from jax.sharding import PartitionSpec as P

MESH = pl.DeviceIdType.MESH
ROWS = 16
LANES = 128
QUARTERS = 4
LESSER, GREATER = 0, 1
DIRECT = 1
AHEAD = 3
AHEAD_TOP = 2
EARLY = 4
LOW_LAG = 8
DONE_LAG = 6
LATE = 3
F32 = jnp.float32
BF16 = jnp.bfloat16


def nn(a, b):
    return jnp.dot(a, b, preferred_element_type=F32)


def nt(a, b):
    return lax.dot_general(a, b, (((1,), (1,)), ((), ())), preferred_element_type=F32)


def fused_kernel(
    n, cells, green_in, sig_l_in, sig_g_in, coulomb_in, out,
    green, sig_l, sig_g, coulomb, send, recv, send_p, low, part, pol, total,
    in_sem, coulomb_sem, sent_sem, arrive_sem, done_sem, halo_send_sem, halo_recv_sem,
):
    me = lax.axis_index("energy")
    cell = lax.axis_index("cell")
    local = green.shape[1]
    norb = green.shape[2]
    width = n // QUARTERS
    half = 2 * width
    quarter, place = me // width, lax.rem(me, width)
    home = jnp.where(quarter == 0, 1, 2)
    strip = norb // width
    row_parts = strip // ROWS
    col_parts = norb // LANES
    chunks = row_parts * col_parts
    straight = min(DIRECT, chunks)
    has_low = cell > 0
    has_high = cell < cells - 1
    offset = {LESSER: 0, GREATER: n + 1}

    def batch(q):
        return jnp.where(q < straight, 0, 1)

    def load(i, e):
        source, held = ((green_in, green), (sig_g_in, sig_g), (sig_l_in, sig_l))[i]
        return pltpu.make_async_copy(source.at[:, e], held.at[:, e], in_sem.at[i, e])

    for e in range(local):
        load(0, e).start()
        load(1, e).start()

    barrier = pltpu.get_barrier_semaphore()

    def greet(other):
        pl.semaphore_signal(barrier, inc=1, device_id={"energy": other}, device_id_type=MESH)

    @pl.loop(1, width)
    def _(k):
        greet(quarter * width + lax.rem(place + k, width))

    def greet_quarter(other):
        @pl.loop(0, width)
        def _(k):
            greet(other * width + k)

    for mine, others in ((0, (1, 2)), (1, (0, 2)), (2, (1, 3)), (3, (2,))):
        @pl.when(quarter == mine)
        def _():
            for other in others:
                greet_quarter(other)

    @pl.when(has_low)
    def _():
        pl.semaphore_signal(barrier, inc=1, device_id={"cell": cell - 1}, device_id_type=MESH)

    @pl.when(has_high)
    def _():
        pl.semaphore_signal(barrier, inc=1, device_id={"cell": cell + 1}, device_id_type=MESH)

    for e in range(local):
        load(2, e).start()
    coulomb_load = pltpu.make_async_copy(coulomb_in, coulomb, coulomb_sem)
    coulomb_load.start()

    def put(value, kind, comp, e):
        value = value.astype(BF16).reshape(width, strip, norb)
        for q in range(chunks):
            c, r = divmod(q, row_parts)
            send[kind, q, :, comp, e] = value[:, r * ROWS:(r + 1) * ROWS, c * LANES:(c + 1) * LANES]

    reach = width * jnp.where(quarter == 1, 2, jnp.where(quarter == 2, 3, 1))

    def meet():
        pl.semaphore_wait(barrier, width - 1 + reach + has_low.astype(jnp.int32) + has_high.astype(jnp.int32))

    pl.when(quarter == 3)(meet)

    def sum_of(count):
        return recv.at[0, 0:count]

    def block_copy(source, kind, q, slot, other, lane):
        return pltpu.make_async_remote_copy(
            src_ref=source, dst_ref=recv.at[q, offset[kind] + slot],
            send_sem=sent_sem.at[batch(q)], recv_sem=arrive_sem.at[lane, q],
            device_id={"energy": other}, device_id_type=MESH,
        )

    @pl.loop(0, local)
    def _(e):
        load(0, e).wait()
        load(1, e).wait()
        g_re, g_im = green[0, e], green[1, e]
        s_re, s_im = sig_g[0, e], sig_g[1, e]
        g_neg = -g_im
        half_re = (nn(g_re, s_re) + nn(g_neg, s_im)).astype(BF16)
        half_im = (nn(g_re, s_im) + nn(g_im, s_re)).astype(BF16)
        put(nt(g_re, half_re) + nt(g_im, half_im), GREATER, 0, e)
        put(nt(g_re, half_im) + nt(g_neg, half_re), GREATER, 1, e)

        @pl.when(quarter == 3)
        def _():
            for q in range(straight):
                @pl.loop(0, width)
                def _(where):
                    pltpu.make_async_remote_copy(
                        src_ref=send.at[GREATER, q, where, :, e], dst_ref=recv.at[q, offset[GREATER] + me, :, e],
                        send_sem=sent_sem.at[batch(q)], recv_sem=arrive_sem.at[0, q],
                        device_id={"energy": home * width + where}, device_id_type=MESH,
                    ).start()

    pl.when(quarter != 3)(meet)


    def exchange(kind, q):
        lane = jnp.where(quarter == 2, 0, 0 if kind == GREATER else 1)

        @pl.loop(1, width)
        def _(k):
            where = lax.rem(place + k, width)
            block_copy(send.at[kind, q, where], kind, q, me, quarter * width + where, lane).start()

    def lane_at_home(kind):
        return jnp.where(quarter == 0, 2 if kind == GREATER else 1, 0)

    def forward_own(kind, q):
        block_copy(send.at[kind, q, place], kind, q, me, home * width + place, lane_at_home(kind)).start()

    def forward_others(kind, q):
        @pl.loop(1, width)
        def _(k):
            slot = quarter * width + lax.rem(place + k, width)
            block_copy(recv.at[q, offset[kind] + slot], kind, q, slot, home * width + place, lane_at_home(kind)).start()

    def arrived(lane, q, count):
        pltpu.make_async_copy(sum_of(count), sum_of(count), arrive_sem.at[lane, q]).wait()

    def direct(kind, q):
        @pl.loop(0, width)
        def _(where):
            block_copy(send.at[kind, q, where], kind, q, me, home * width + where, lane_at_home(kind)).start()

    ahead = jnp.where(quarter == 3, min(AHEAD_TOP, chunks), min(AHEAD, chunks))
    first = jnp.where(quarter == 3, straight, 0)

    @pl.when(quarter == 1)
    def _():
        @pl.loop(0, straight)
        def _(q):
            direct(GREATER, q)

    @pl.when(quarter != 2)
    def _():
        @pl.loop(jnp.where(quarter == 0, 0, straight), ahead)
        def _(q):
            forward_own(GREATER, q)

    @pl.loop(first, ahead)
    def _(q):
        exchange(GREATER, q)

    @pl.loop(0, local)
    def _(e):
        load(2, e).wait()
        g_re, g_im = green[0, e], green[1, e]
        l_re, l_im = sig_l[0, e], sig_l[1, e]
        g_neg = -g_im
        half_re = (nn(g_re, l_re) + nn(g_neg, l_im)).astype(BF16)
        half_im = (nn(g_re, l_im) + nn(g_im, l_re)).astype(BF16)
        put(nt(half_re, g_re) + nt(half_im, g_im), LESSER, 0, e)
        put(nt(half_im, g_re) + nt(half_re, g_neg), LESSER, 1, e)

    @pl.when(quarter == 3)
    def _():
        @pl.loop(0, straight)
        def _(q):
            direct(LESSER, q)

        @pl.loop(straight, ahead)
        def _(q):
            forward_own(LESSER, q)

    @pl.loop(first, ahead)
    def _(q):
        exchange(LESSER, q)

    @pl.loop(ahead, jnp.where(jnp.logical_or(quarter == 1, quarter == 2), min(EARLY, chunks), chunks))
    def _(q):
        exchange(GREATER, q)
        exchange(LESSER, q)

    def more(t):
        @pl.when(t + EARLY < chunks)
        def _():
            exchange(GREATER, t + EARLY)
            exchange(LESSER, t + EARLY)

    blank = jnp.zeros((2, local, ROWS, LANES), BF16)

    @pl.when(quarter != 3)
    def _():
        @pl.loop(0, chunks)
        def _(q):
            for kind in (LESSER, GREATER):
                recv[q, offset[kind] + me] = send[kind, q, place]

    @pl.when(quarter == 1)
    def _():
        @pl.loop(0, chunks)
        def _(q):
            recv[q, width - 1] = blank
            recv[q, half] = blank

    @pl.when(quarter == 0)
    def _():
        @pl.loop(0, chunks)
        def _(q):
            recv[q, width] = blank

    @pl.when(quarter == 2)
    def _():
        @pl.loop(0, chunks)
        def _(q):
            recv[q, half - 1] = blank
            recv[q, n] = blank

    def spot(q):
        rows = pl.ds(pl.multiple_of(lax.rem(q, row_parts) * ROWS, ROWS), ROWS)
        return rows, pl.ds(pl.multiple_of(q // row_parts * LANES, LANES), LANES)

    def return_copy(q, owner):
        return pltpu.make_async_remote_copy(
            src_ref=send_p.at[q, owner], dst_ref=pol.at[1, :, :, place, *spot(q)],
            send_sem=sent_sem.at[batch(q)], recv_sem=done_sem.at[q],
            device_id={"energy": owner}, device_id_type=MESH,
        )

    def low_copy(q, owner):
        return pltpu.make_async_remote_copy(
            src_ref=send_p.at[q, owner], dst_ref=low.at[q, place],
            send_sem=sent_sem.at[batch(q)], recv_sem=done_sem.at[q],
            device_id={"energy": owner}, device_id_type=MESH,
        )

    def halo_copy(q, slot, other):
        return pltpu.make_async_remote_copy(
            src_ref=pol.at[1, :, :, :, *spot(q)], dst_ref=pol.at[slot, :, :, :, *spot(q)],
            send_sem=halo_send_sem.at[slot // 2], recv_sem=halo_recv_sem.at[slot // 2, q // row_parts],
            device_id={"cell": other}, device_id_type=MESH,
        )

    factor = 1.0 / math.sqrt(n * local)

    def correlate(q, b, first_step, last_step, extra=None):
        def step(a, acc):
            first = [
                (recv[q, a + b + i // local, 0, i % local].astype(F32), recv[q, a + b + i // local, 1, i % local].astype(F32))
                for i in range(2 * local - 1)
            ]
            acc = list(acc)
            for e in range(local):
                x_re, x_im = recv[q, n + 1 + a, 0, e].astype(F32), recv[q, n + 1 + a, 1, e].astype(F32)
                for w in range(local):
                    y_re, y_im = first[e + w]
                    acc[2 * w] = acc[2 * w] + (y_re * x_re - y_im * x_im)
                    acc[2 * w + 1] = acc[2 * w + 1] + (y_re * x_im + y_im * x_re)
            return tuple(acc)

        zero = jnp.zeros((ROWS, LANES), F32)
        acc = lax.fori_loop(first_step, last_step, step, (zero,) * (2 * local))
        for w in range(local):
            for c in range(2):
                value = acc[2 * w + c] * factor
                if extra is not None:
                    value = value + extra[q, b, c, w].astype(F32)
                send_p[q, b, c, w] = value.astype(BF16)

    def halo(q):
        @pl.when(has_low)
        def _():
            halo_copy(q, 2, cell - 1).start()

        @pl.when(has_high)
        def _():
            halo_copy(q, 0, cell + 1).start()

    def done(q, count):
        pltpu.make_async_copy(sum_of(count), sum_of(count), done_sem.at[q]).wait()

    def finish(q, count):
        done(q, count)

        @pl.loop(0, width)
        def _(where):
            for c in range(2):
                for w in range(local):
                    place_of = (1, c, w, where, *spot(q))
                    pol[place_of] = (pol[place_of].astype(F32) + low[q, where, c, w].astype(F32)).astype(BF16)

        halo(q)

    @pl.when(jnp.logical_not(has_low))
    def _():
        pol[0] = jnp.zeros_like(pol[0])

    @pl.when(jnp.logical_not(has_high))
    def _():
        pol[2] = jnp.zeros_like(pol[2])

    def low_out(q, b):
        @pl.when(b != me)
        def _():
            low_copy(q, b).start()

        @pl.when(b == me)
        def _():
            low[q, place] = send_p[q, b]

    def part_copy(q, b):
        return pltpu.make_async_remote_copy(
            src_ref=send_p.at[q, b], dst_ref=part.at[q, b],
            send_sem=sent_sem.at[batch(q)], recv_sem=arrive_sem.at[2, q],
            device_id={"energy": place}, device_id_type=MESH,
        )

    @pl.when(quarter == 0)
    def _():
        @pl.loop(0, chunks)
        def _(t):
            if width > 1:
                arrived(0, t, width - 1)
            forward_others(GREATER, t)

            @pl.when(t + ahead < chunks)
            def _():
                forward_own(GREATER, t + ahead)

        @pl.loop(0, chunks + LOW_LAG)
        def _(t):
            @pl.when(t < chunks)
            def _():
                if width > 1:
                    arrived(1, t, width - 1)
                arrived(2, t, width)

                @pl.loop(0, width)
                def _(b):
                    correlate(t, b, 0, width - b, part)
                    low_out(t, b)

            @pl.when(t >= LOW_LAG)
            def _():
                finish(t - LOW_LAG, 2 * width - 1)

    @pl.when(quarter == 1)
    def _():
        @pl.loop(0, chunks + DONE_LAG)
        def _(t):
            @pl.when(t < chunks)
            def _():
                if width > 1:
                    arrived(0, t, width - 1)

                @pl.when(t >= straight)
                def _():
                    forward_others(GREATER, t)

                arrived(2, t, width)
                lower = recv.at[t, n + 1:n + 1 + width]
                pltpu.make_async_remote_copy(
                    src_ref=lower, dst_ref=lower, send_sem=sent_sem.at[batch(t)], recv_sem=arrive_sem.at[0, t],
                    device_id={"energy": 2 * width + place}, device_id_type=MESH,
                ).start()
                more(t)

            @pl.when(t + ahead < chunks)
            def _():
                forward_own(GREATER, t + ahead)

            @pl.when(t < chunks)
            def _():
                if width > 1:
                    arrived(1, t, width - 1)

                @pl.loop(0, half)
                def _(b):
                    correlate(t, b, jnp.maximum(width - 1 - b, 0), half - b)

                    @pl.when(b < width)
                    def _():
                        part_copy(t, b).start()

                    @pl.when(b >= width)
                    def _():
                        low_out(t, b)

            @pl.when(t >= DONE_LAG)
            def _():
                finish(t - DONE_LAG, 2 * width - 1)

    @pl.when(quarter == 2)
    def _():
        @pl.loop(0, chunks + LATE)
        def _(t):
            @pl.when(t < chunks)
            def _():
                arrived(0, t, 6 * width - 2)
                more(t)

                @pl.loop(0, n)
                def _(b):
                    correlate(t, b, jnp.maximum(half - 1 - b, 0), n - b)

                    @pl.when(b != me)
                    def _():
                        return_copy(t, b).start()

                    @pl.when(b == me)
                    def _():
                        pol[1, :, :, place, *spot(t)] = send_p[t, b]

            @pl.when(t >= LATE)
            def _():
                if width > 1:
                    done(t - LATE, width - 1)
                halo(t - LATE)

    @pl.when(quarter == 3)
    def _():
        @pl.loop(straight, chunks)
        def _(t):
            for kind in (GREATER, LESSER):
                if width > 1:
                    arrived(0 if kind == GREATER else 1, t, width - 1)
                forward_others(kind, t)

            @pl.when(t + ahead - straight < chunks)
            def _():
                forward_own(GREATER, t + ahead - straight)
                forward_own(LESSER, t + ahead - straight)

        @pl.loop(0, chunks)
        def _(q):
            done(q, width)
            halo(q)

    coulomb_load.wait()

    def polarized(slot, e, part):
        cols = slice(part * LANES, (part + 1) * LANES)
        return jnp.concatenate([pol[slot, c, e, :, :, cols].reshape(norb, LANES) for c in range(2)], 1)

    last = col_parts - 1

    @pl.loop(0, local)
    def _(e):
        total[e] = nn(coulomb[1], polarized(1, e, last))

    near = jnp.where(lax.rem(cell, 2) == 0, 2, 0)

    def halo_arrived(slot, part):
        group = (slice(None), slice(None), slice(None), slice(None), slice(part * LANES, (part + 1) * LANES))

        @pl.when(jnp.where(slot == 0, cell, cells - 1 - cell) > 0)
        def _():
            pltpu.make_async_copy(pol.at[slot, *group], pol.at[slot, *group], halo_recv_sem.at[slot // 2, part]).wait()

    for part_of in range(col_parts):
        cols = slice(part_of * LANES, (part_of + 1) * LANES)
        halo_arrived(near, part_of)

        if part_of == last:
            @pl.loop(0, local)
            def _(e):
                total[e] = total[e] + nn(coulomb[near], polarized(near, e, part_of))

        halo_arrived(2 - near, part_of)

        @pl.loop(0, local)
        def _(e):
            if part_of == last:
                summed = total[e]
            else:
                summed = nn(coulomb[1], polarized(1, e, part_of)) + nn(coulomb[near], polarized(near, e, part_of))
            summed = nn(coulomb[2 - near], polarized(2 - near, e, part_of)) + summed
            for c in range(2):
                out[c, e, :, cols] = summed[:, c * LANES:(c + 1) * LANES].astype(BF16)

    @pl.when(has_low)
    def _():
        pltpu.make_async_copy(pol.at[1], pol.at[1], halo_send_sem.at[1]).wait()

    @pl.when(has_high)
    def _():
        pltpu.make_async_copy(pol.at[1], pol.at[1], halo_send_sem.at[0]).wait()

    def all_sent(*counts):
        for i, (count, size) in enumerate(zip(counts, (straight, chunks - straight))):
            if count * size:
                sent = recv.at[0:size, 0:count]
                pltpu.make_async_copy(sent, sent, sent_sem.at[i]).wait()

    @pl.when(quarter == 0)
    def _():
        all_sent(4 * width - 3, 4 * width - 3)

    @pl.when(quarter == 3)
    def _():
        all_sent(2 * width, 4 * width - 2)

    @pl.when(jnp.logical_or(quarter == 1, quarter == 2))
    def _():
        all_sent(6 * width - 3, 6 * width - 3)


def fused(n, cells, retarded, sigma_lesser, sigma_greater, coulomb):
    green = retarded[0]
    local, norb = green.shape[1], green.shape[2]
    width = n // QUARTERS
    strip = norb // width
    chunks = strip // ROWS * (norb // LANES)
    dma = pltpu.SemaphoreType.DMA
    result = pl.pallas_call(
        functools.partial(fused_kernel, n, cells),
        out_shape=pltpu.VMEM(green.shape, BF16),
        in_specs=[pl.BlockSpec(memory_space=pltpu.HBM)] * 4,
        out_specs=pl.BlockSpec(memory_space=pltpu.VMEM),
        scratch_shapes=[
            pltpu.VMEM(green.shape, BF16),
            pltpu.VMEM(green.shape, BF16),
            pltpu.VMEM(green.shape, BF16),
            pltpu.VMEM(coulomb.shape[1:], BF16),
            pltpu.VMEM((2, chunks, width, 2, local, ROWS, LANES), BF16),
            pltpu.VMEM((chunks, 2 * n + 1, 2, local, ROWS, LANES), BF16),
            pltpu.VMEM((chunks, n, 2, local, ROWS, LANES), BF16),
            pltpu.VMEM((chunks, width, 2, local, ROWS, LANES), BF16),
            pltpu.VMEM((chunks, width, 2, local, ROWS, LANES), BF16),
            pltpu.VMEM((3, 2, local, width, strip, norb), BF16),
            pltpu.VMEM((local, norb, 2 * LANES), F32),
            dma((3, local)), dma,
            dma((2,)), dma((3, chunks)), dma((chunks,)),
            dma((2,)), dma((2, norb // LANES)),
        ],
        compiler_params=pltpu.CompilerParams(
            collective_id=0, has_side_effects=True, vmem_limit_bytes=56 * 1024 * 1024
        ),
    )(green, sigma_lesser[0], sigma_greater[0], coulomb[0])
    return result[None]


def thin(n, cells, retarded, sigma_lesser, sigma_greater, coulomb):
    green = retarded[0]
    local = green.shape[1]

    def halves(sigma):
        def product(x, y):
            return jnp.einsum("eik,ekj->eij", x, y, preferred_element_type=F32)

        re = product(green[0], sigma[0]) - product(green[1], sigma[1])
        im = product(green[0], sigma[1]) + product(green[1], sigma[0])
        return re.astype(BF16), im.astype(BF16)

    def adjoint(x, y):
        return jnp.einsum("eik,ejk->eij", x, y, preferred_element_type=F32)

    re, im = halves(sigma_lesser[0])
    lesser = jnp.stack([adjoint(re, green[0]) + adjoint(im, green[1]), adjoint(im, green[0]) - adjoint(re, green[1])])
    re, im = halves(sigma_greater[0])
    greater = jnp.stack([adjoint(green[0], re) + adjoint(green[1], im), adjoint(green[0], im) - adjoint(green[1], re)])
    first = lax.all_to_all(lesser.astype(BF16), "energy", split_axis=2, concat_axis=1, tiled=True).astype(F32)
    second = lax.all_to_all(greater.astype(BF16), "energy", split_axis=2, concat_axis=1, tiled=True).astype(F32)
    energies = n * local
    padded = jnp.concatenate([first, jnp.zeros_like(first)], axis=1)

    def lag(w):
        y = lax.dynamic_slice_in_dim(padded, w, energies, axis=1)
        re = jnp.sum(y[0] * second[0] - y[1] * second[1], axis=0)
        im = jnp.sum(y[0] * second[1] + y[1] * second[0], axis=0)
        return (jnp.stack([re, im]) / math.sqrt(energies)).astype(BF16)

    polarized = jnp.swapaxes(lax.map(lag, jnp.arange(energies)), 0, 1)
    polarized = lax.all_to_all(polarized, "energy", split_axis=1, concat_axis=2, tiled=True)
    up = [(i, i + 1) for i in range(cells - 1)]
    low = lax.ppermute(polarized, "cell", up)
    high = lax.ppermute(polarized, "cell", [(t, s) for s, t in up])
    stacked = jnp.stack([low, polarized, high])
    summed = jnp.einsum("dik,dcekj->ceij", coulomb[0], stacked, preferred_element_type=F32)
    return summed.astype(BF16)[None]


def solution(mesh):
    n, cells = mesh.shape["energy"], mesh.shape["cell"]

    def on_device(retarded, sigma_lesser, sigma_greater, coulomb):
        norb = retarded.shape[-1]
        whole_tiles = n % QUARTERS == 0 and norb % LANES == 0 and norb % (n // QUARTERS * ROWS) == 0
        plan = fused if whole_tiles else thin
        return plan(n, cells, retarded, sigma_lesser, sigma_greater, coulomb)

    in_specs = (
        P("cell", None, "energy", None, None),
        P("cell", None, "energy", None, None),
        P("cell", None, "energy", None, None),
        P("cell", None, None, None),
    )
    out_specs = P("cell", None, "energy", None, None)
    return jax.shard_map(
        on_device, mesh=mesh, in_specs=in_specs, out_specs=out_specs, check_vma=False
    )
```
